128 devices in a mesh: fsdp: 16 (over z, x_lo, core), rows: 8 (over y, x_hi).
Axes of the slice: x: 4 (x_hi: 2, x_lo: 2; x = x_hi * 2 + x_lo), y: 4, z: 4, core: 2. Of those that a mesh axis runs over, the one named last changes fastest.
Arguments:
- query_rows: bfloat16 [16, 2048, 1536], P('fsdp', 'rows'), may hold values from -6 to 6
- key_rows: bfloat16 [16, 2048, 1536], P('fsdp', 'rows'), may hold values from -6 to 6
- value_rows: bfloat16 [16, 2048, 1536], P('fsdp', 'rows'), may hold values from -6 to 6
- grad_out: bfloat16 [16, 2048, 3072], P('fsdp', 'rows'), may hold values from -6 to 6
- w_out: bfloat16 [1536, 3072], P('fsdp'), may hold values from -0.15625 to 0.15625
Outputs:
- grad_query: bfloat16 [16, 2048, 1536], P('fsdp', 'rows')
- grad_key: bfloat16 [16, 2048, 1536], P('fsdp', 'rows')
- grad_value: bfloat16 [16, 2048, 1536], P('fsdp', 'rows')
- grad_w_out: float32 [1536, 3072], P('fsdp')
The draws below stay inside these ranges and needn't reach their ends.
All inputs are finite; a program needn't handle non-finite values.
Results may differ from the reference program's by a relative error of at most 0.02.
Values may be sent and summed in bfloat16 or wider, within the bound.
A program may use at most 192 MiB of HBM per device.

```python
import math
import jax
import jax.numpy as jnp
from jax import lax

D = 3072
HDIM = 128
HEADS = 12
TOK_DEV = 256
HW = 1536
SEQ = 2048
IMAGES = 16
N_ROWS = 8


def drawn(key):
    base = jax.random.fold_in(key, 11)
    key_query, key_keys = jax.random.split(base, 2)
    shape = (IMAGES, SEQ, HW)
    query = jnp.clip(jax.random.normal(key_query, shape, jnp.float32), -6.0, 6.0)
    keys_out = jnp.clip(jax.random.normal(key_keys, shape, jnp.float32), -6.0, 6.0)
    return (query.astype(jnp.bfloat16), keys_out.astype(jnp.bfloat16))


def draw_query_rows(key, part):
    return drawn(key)[0]


def draw_key_rows(key, part):
    return drawn(key)[1]


def strengthened(result, key, source, target, parts, factor):
    owner, partner = [(jnp.arange(result.shape[dim]) // (result.shape[dim] // parts)).reshape([-1 if axis == dim else 1 for axis in range(result.ndim)]) for dim in (source, target)]
    chosen = jax.random.permutation(key, parts)[partner]
    strong = (owner == chosen) | (owner == (partner + parts // 2) % parts)
    return jnp.where(strong, factor * result, result)


def levels(stream_key, dims, pieces, least, largest):
    level, own = 1.0, jax.random.fold_in(stream_key, 6)
    for axis_at, blocks in pieces:
        steps = jnp.exp(jax.random.uniform(jax.random.fold_in(own, axis_at), (blocks,), jnp.float32, least / len(pieces), largest / len(pieces)))
        level = level * jnp.repeat(steps, dims[axis_at] // blocks).reshape([-1 if axis == axis_at else 1 for axis in range(len(dims))])
    return level


def bell_draw(stream_key, extent, width, most, shards=(), held_as=jnp.bfloat16):
    entries = jax.random.normal(stream_key, extent, jnp.float32) * width
    if len(shards) > 0:
        entries = levels(stream_key, extent, shards, -0.22, 0.18) * entries
    return jnp.clip(entries, min=-most, max=most).astype(held_as)


def noise_with(own_key, extent, deviation, most, cuts, heavy, held_as=jnp.bfloat16):
    array = deviation * jax.random.normal(own_key, extent, jnp.float32)
    if cuts:
        array = array * levels(own_key, extent, cuts, -0.22, 0.18)
    return jnp.clip(strengthened(array, jax.random.fold_in(own_key, 3), *heavy), -most, most).astype(held_as)


def setup_inputs(seed: int = 0) -> dict:
    key_of = jax.random.split(jax.random.key(seed), 6)
    return {
        "query_rows": draw_query_rows(jax.random.fold_in(key_of[5], 71), 0),
        "key_rows": draw_key_rows(jax.random.fold_in(key_of[5], 71), 0),
        "value_rows": noise_with(key_of[2], (IMAGES, SEQ, HW), 1.0, 6.0, ((0, 16), (1, 8)), (0, 2, 16, 2.0)),
        "grad_out": bell_draw(key_of[3], (IMAGES, SEQ, D), 1.0, 6.0, ((0, 16), (1, 8))),
        "w_out": bell_draw(key_of[4], (HW, D), HW ** -0.5, 0.15625, ((0, 16),)),
    }


def one_image(inputs, w_out):
    query, key_in, value, grad_img = inputs
    factor = 1.0 / math.sqrt(HDIM)
    query_f = query.astype(jnp.float32).reshape(N_ROWS, TOK_DEV, HEADS, HDIM)
    key_f = key_in.astype(jnp.float32).reshape(SEQ, HEADS, HDIM)
    value_f = value.astype(jnp.float32).reshape(SEQ, HEADS, HDIM)
    scores = jnp.einsum('rqhd,khd->rhqk', query_f, key_f) * factor
    probs = jax.nn.softmax(scores, axis=-1)
    probs_low = lax.optimization_barrier(probs.astype(jnp.bfloat16)).astype(jnp.float32)
    attended = jnp.einsum('rhqk,khd->rqhd', probs_low, value_f).astype(jnp.bfloat16).reshape(SEQ, HW)
    grad_attn = jnp.dot(grad_img, w_out.T, preferred_element_type=jnp.float32).astype(jnp.bfloat16)
    grad_heads = lax.optimization_barrier(grad_attn).astype(jnp.float32).reshape(N_ROWS, TOK_DEV, HEADS, HDIM)
    value_part = jnp.einsum('rhqk,rqhd->rkhd', probs_low, grad_heads)
    value_part = lax.optimization_barrier(value_part.astype(jnp.bfloat16)).astype(jnp.float32)
    grad_value = lax.optimization_barrier(jnp.sum(value_part, axis=0)).astype(jnp.bfloat16).reshape(SEQ, HW)
    grad_probs = jnp.einsum('rqhd,khd->rhqk', grad_heads, value_f)
    centre = lax.optimization_barrier(jnp.sum(probs * grad_probs, axis=-1, keepdims=True))
    grad_scores = lax.optimization_barrier((probs * (grad_probs - centre)).astype(jnp.bfloat16)).astype(jnp.float32)
    grad_query = (jnp.einsum('rhqk,khd->rqhd', grad_scores, key_f) * factor).astype(jnp.bfloat16).reshape(SEQ, HW)
    key_part = jnp.einsum('rhqk,rqhd->rkhd', grad_scores, query_f) * factor
    key_part = lax.optimization_barrier(key_part.astype(jnp.bfloat16)).astype(jnp.float32)
    grad_key = lax.optimization_barrier(jnp.sum(key_part, axis=0)).astype(jnp.bfloat16).reshape(SEQ, HW)
    attended_blocks = lax.optimization_barrier(attended).astype(jnp.float32).reshape(N_ROWS, TOK_DEV, HW)
    grad_blocks = grad_img.astype(jnp.float32).reshape(N_ROWS, TOK_DEV, D)
    block_terms = jnp.einsum('rti,rtd->rid', attended_blocks, grad_blocks)
    block_terms = lax.optimization_barrier(block_terms.astype(jnp.bfloat16)).astype(jnp.float32)
    grad_weight = lax.optimization_barrier(jnp.sum(block_terms, axis=0))
    return (grad_query, grad_key, grad_value, grad_weight)

def reference(query_rows, key_rows, value_rows, grad_out, w_out):
    grad_query, grad_key, grad_value, grad_weight = lax.map(lambda inputs: one_image(inputs, w_out), (query_rows, key_rows, value_rows, grad_out))
    return (grad_query, grad_key, grad_value, lax.optimization_barrier(jnp.sum(grad_weight, axis=0)))
```

```python
import math

import jax
import jax.numpy as jnp
from jax import lax
from jax.experimental import pallas as pl
from jax.experimental.pallas import tpu as pltpu
from jax.sharding import PartitionSpec as P

F32 = jnp.float32
BF16 = jnp.bfloat16
MESH = pl.DeviceIdType.MESH
D = 3072
HW = 1536
HD = 128
TOK = 256
GW = 384
SEQ = 2048
HALF = 1024
KC = 256
NK = SEQ // KC
SCALE = 1.0 / math.sqrt(HD)
CST = SCALE * math.log2(math.e)


def m128(x):
    return pl.multiple_of(x, 128)


def m256(x):
    return pl.multiple_of(x, 256)


def local_copy(src, dst, sem):
    return pltpu.make_async_copy(src, dst, sem)


def remote(src, dst, send_sem, recv_sem, dev):
    return pltpu.make_async_remote_copy(
        src_ref=src, dst_ref=dst, send_sem=send_sem, recv_sem=recv_sem,
        device_id=dev, device_id_type=MESH,
    )


def landed(ref, sem):
    pltpu.make_async_copy(ref, ref, sem).wait()


def dot(a, b):
    return jnp.dot(a, b, preferred_element_type=F32)


def kernel(
    q_hbm, k_hbm, v_hbm, go_hbm, w_hbm,
    gq_out, gk_out, gv_out, gw_out,
    qbuf, kbuf, vbuf, ktb, vtb, go, wbuf, sbuf, pbuf, gat, att, obuf, linv,
    dkacc, dvacc, termb, rsb, redb, gwb, gqb, pk, xbuf, keep, fin,
    ss1, rs1, ls1, ss2, rs2, ss3, rs3, lsg, ssw1, rsw1, ssw2, rsw2,
    ss5, rs5, ss6, rs6, ss7, rs7, ls7, ss8, rs8, ss9, rs9, ls9,
):
    f = lax.axis_index("fsdp")
    r = lax.axis_index("rows")
    z, xl, c = f // 4, (f // 2) % 2, f % 2
    y, xh = r // 2, r % 2
    j = f % 4

    def dev(z_, xl_, c_, y_, xh_):
        return (z_ * 4 + xl_ * 2 + c_, y_ * 2 + xh_)

    def ydev(y_):
        return dev(z, xl, c, y_, xh)

    partner = dev(z, xl, c, y, 1 - xh)
    ins = (k_hbm, v_hbm, q_hbm)

    def slot(t, hh, ys):
        if t == 2:
            return qbuf.at[hh, pl.ds(m256(ys * TOK), TOK), :]
        return (kbuf, vbuf)[t].at[hh, pl.ds(m256((xh * 4 + ys) * TOK), TOK), :]

    def cols(t, hh, yd):
        return ins[t].at[0, :, pl.ds(m128(yd * GW + hh * HD), HD)]

    w_own = wbuf.at[pl.ds(pl.multiple_of(j * 96, 32), 96), :]

    @pl.when(z == y)
    def _():
        local_copy(w_hbm, w_own, rsw1.at[0]).start()
        for dz in (1, 2, 3):
            remote(w_hbm, w_own, ssw1.at[dz - 1], rsw1.at[0], dev((z + dz) % 4, xl, c, y, xh)).start()

    def send_head(hh, carry):
        for t in range(3):
            for d in (1, 3, 2):
                yd = (y + d) % 4
                i = (hh * 3 + t) * 3 + d - 1
                remote(cols(t, hh, yd), slot(t, hh, y), ss1.at[i], rs1.at[i], ydev(yd)).start()
            local_copy(cols(t, hh, y), slot(t, hh, y), ls1.at[hh * 3 + t]).start()
        return carry

    lax.fori_loop(0, 3, send_head, 0)

    def go_slot(ys, h, n=1):
        return go.at[pl.ds(pl.multiple_of(ys * TOK + h * 128, 128), 128 * n), :]

    def go_src(h):
        return go_hbm.at[0, pl.ds(h * 128, 128), :]

    yr, yl = (y + 1) % 4, (y + 3) % 4
    yo = (y + 2) % 4
    remote(go_src(0), go_slot(y, 0), ss3.at[0], rs3.at[0], ydev(yr)).start()
    remote(go_src(1), go_slot(y, 1), ss3.at[2], rs3.at[2], ydev(yl)).start()
    remote(go_src(1), go_slot(y, 1), ss3.at[1], rs3.at[1], ydev(yr)).start()
    remote(go_src(0), go_slot(y, 0), ss3.at[3], rs3.at[3], ydev(yl)).start()
    local_copy(go_hbm.at[0], go_slot(y, 0, 2), lsg.at[0]).start()

    def kv_half(t, hh, h):
        return (kbuf, vbuf)[t].at[hh, pl.ds(m256(h * HALF), HALF), :]

    def relay(hh, carry):
        for t in range(2):
            local_copy(cols(t, hh, y), slot(t, hh, y), ls1.at[hh * 3 + t]).wait()
            for d in (1, 3, 2):
                i = (hh * 3 + t) * 3 + d - 1
                landed(slot(t, hh, (y + 4 - d) % 4), rs1.at[i])
            i = hh * 2 + t
            half = kv_half(t, hh, xh)
            remote(half, half, ss2.at[i], rs2.at[i], partner).start()
        return carry

    lax.fori_loop(0, 3, relay, 0)

    landed(w_own, rsw1.at[0])
    for n in (1, 2, 3):
        a, b = n // 2, n % 2
        remote(w_own, w_own, ssw2.at[n - 1], rsw2.at[n - 1],
               dev(z, (xl + a) % 2, (c + b) % 2, y, xh)).start()

    def forward(hh, carry):
        for t in range(2):
            landed(kv_half(t, hh, 1 - xh), rs2.at[hh * 2 + t])
        local_copy(cols(2, hh, y), slot(2, hh, y), ls1.at[hh * 3 + 2]).wait()
        for d in (1, 3, 2):
            landed(slot(2, hh, (y + 4 - d) % 4), rs1.at[(hh * 3 + 2) * 3 + d - 1])
        for kc in range(NK):
            ks = slice(kc * KC, (kc + 1) * KC)
            ktb[hh, :, ks] = kbuf[hh, ks, :].T
            vtb[hh, :, ks] = vbuf[hh, ks, :].T

        def block(qb, carry):
            i = hh * 4 + qb
            qs = pl.ds(m256(qb * TOK), TOK)
            qt = qbuf[hh, qs, :].T
            m = jnp.full((1, TOK), -jnp.inf, F32)
            for kc in range(NK):
                ks = slice(kc * KC, (kc + 1) * KC)
                s = dot(kbuf[hh, ks, :], qt)
                sbuf[ks, :] = s
                m = jnp.maximum(m, jnp.max(s, axis=0, keepdims=True))
            mc = m * CST
            l = jnp.zeros((1, TOK), F32)
            o = jnp.zeros((HD, TOK), F32)
            for kc in range(NK):
                ks = slice(kc * KC, (kc + 1) * KC)
                p = jnp.exp2(sbuf[ks, :] * CST - mc)
                l = l + jnp.sum(p, axis=0, keepdims=True)
                pb = p.astype(BF16)
                pbuf[i, ks, :] = pb
                o = o + dot(vtb[hh, :, ks], pb)
            inv = 1.0 / l
            on = o * inv
            obuf[i] = on
            att[pl.ds(m128(hh * HD), HD), qs] = on.astype(BF16)
            linv[i] = jnp.broadcast_to(inv, (8, TOK))
            return carry

        return lax.fori_loop(0, 4, block, carry)

    forward(0, 0)

    landed(go_slot(yl, 0), rs3.at[0])
    remote(go_slot(yl, 0), go_slot(yl, 0), ss3.at[4], rs3.at[4], ydev(yr)).start()
    landed(go_slot(yr, 1), rs3.at[2])
    remote(go_slot(yr, 1), go_slot(yr, 1), ss3.at[5], rs3.at[5], ydev(yl)).start()

    lax.fori_loop(1, 3, forward, 0)

    for n in (1, 2, 3):
        a, b = n // 2, n % 2
        jn = ((xl + a) % 2) * 2 + (c + b) % 2
        landed(wbuf.at[pl.ds(pl.multiple_of(jn * 96, 32), 96), :], rsw2.at[n - 1])

    def project(ys):
        rows = pl.ds(m256(ys * TOK), TOK)
        g = lax.dot_general(wbuf[...], go[rows, :], (((1,), (1,)), ((), ())), preferred_element_type=F32)
        gat[ys] = g.astype(BF16)

    local_copy(go_hbm.at[0], go_slot(y, 0, 2), lsg.at[0]).wait()
    landed(go_slot(yl, 1), rs3.at[1])
    landed(go_slot(yr, 0), rs3.at[3])
    landed(go_slot(yo, 0), rs3.at[4])
    landed(go_slot(yo, 1), rs3.at[5])

    def project_all(d, carry):
        project((y + d) % 4)
        return carry

    lax.fori_loop(0, 4, project_all, 0)

    def term(o, carry):
        zd, xd = (z + o // 2) % 4, (xh + o % 2) % 2
        col = zd * 2 + xd
        cs = pl.ds(m128(col * GW), GW)
        termb[col] = dot(att[...], go[:, cs]).astype(BF16)
        for n in range(4):
            a, b = n // 2, n % 2
            xld, cd = (xl + a) % 2, (c + b) % 2
            jd = xld * 2 + cd
            piece = termb.at[col, pl.ds(pl.multiple_of(jd * 96, 32), 96), :]
            i = o * 4 + n

            def go_out():
                remote(piece, rsb.at[i], ss5.at[i], rs5.at[i], dev(zd, xld, cd, y, xd)).start()

            if n == 0:
                pl.when(o > 0)(go_out)
            else:
                go_out()
        return carry

    lax.fori_loop(0, 8, term, 0)

    def back_slot(out, hh, yd, ysrc):
        del yd
        return out.at[0, :, pl.ds(m128(ysrc * GW + hh * HD), HD)]

    def hand_out(buf, out, hh, ss, rs, ls, base, lbase):
        for d in (1, 3, 2):
            yd = (y + d) % 4
            remote(buf(yd), back_slot(out, hh, yd, y), ss.at[base + d - 1], rs.at[base + d - 1], ydev(yd)).start()
        local_copy(buf(y), back_slot(out, hh, y, y), ls.at[lbase]).start()

    def finish_kv(hh):
        for t in range(2):
            i = hh * 2 + t
            landed(xbuf.at[i], rs8.at[i])
            fin[i] = (keep[i] + xbuf[i].astype(F32)).astype(BF16)
            hand_out(
                lambda yd: fin.at[i, pl.ds(m256(yd * TOK), TOK), :],
                (gk_out, gv_out)[t], hh, ss9, rs9, ls9, i * 3, i,
            )

    def backward(hh, carry):
        dkacc[...] = jnp.zeros_like(dkacc)
        dvacc[...] = jnp.zeros_like(dvacc)

        def block(qb, carry):
            i = hh * 4 + qb
            qs = pl.ds(m256(qb * TOK), TOK)
            qn = qbuf[hh, qs, :]
            inv = linv[i][0:1, :]
            gt = (gat[qb, pl.ds(m128(hh * HD), HD), :].astype(F32) * inv).astype(BF16)
            gn = gt.T
            cen = jnp.sum(gt.astype(F32) * obuf[i], axis=0, keepdims=True)
            dq = jnp.zeros((HD, TOK), F32)
            for kc in range(NK):
                ks = slice(kc * KC, (kc + 1) * KC)
                dp = dot(vbuf[hh, ks, :], gt)
                pb = pbuf[i, ks, :]
                ds = (pb.astype(F32) * (dp - cen)).astype(BF16)
                dq = dq + dot(ktb[hh, :, ks], ds)
                dkacc[ks, :] += dot(ds, qn)
                dvacc[ks, :] += dot(pb, gn)
            gqb[hh, qs, :] = (dq * SCALE).T.astype(BF16)
            return carry

        lax.fori_loop(0, 4, block, 0)
        mine, other = pl.ds(m256(xh * HALF), HALF), pl.ds(m256((1 - xh) * HALF), HALF)
        for t in range(2):
            acc = (dkacc, dvacc)[t]
            fac = (SCALE, 1.0)[t]
            i = hh * 2 + t
            pk[i] = (acc[other, :] * fac).astype(BF16)
            remote(pk.at[i], xbuf.at[i], ss8.at[i], rs8.at[i], partner).start()
            keep[i] = acc[mine, :] * fac
        hand_out(lambda yd: gqb.at[hh, pl.ds(m256(yd * TOK), TOK), :], gq_out, hh, ss7, rs7, ls7, hh * 3, hh)

        @pl.when(hh > 0)
        def _():
            finish_kv(hh - 1)

        return carry

    lax.fori_loop(0, 3, backward, 0)

    own = z * 2 + xh
    acc = termb[own, pl.ds(pl.multiple_of(j * 96, 32), 96), :].astype(F32)

    def add(i, acc):
        landed(rsb.at[i], rs5.at[i])
        return acc + rsb[i].astype(F32)

    redb[...] = lax.fori_loop(1, 32, add, acc).astype(BF16)
    for n in range(8):
        d, e = n // 2, n % 2
        yd, xd = (y + d) % 4, (xh + e) % 2

        def out_remote():
            remote(redb, gwb.at[own], ss6.at[n], rs6.at[own], dev(y, xl, c, yd, xd)).start()

        if n == 0:
            pl.when(z != y)(out_remote)

            @pl.when(z == y)
            def _():
                local_copy(redb, gwb.at[own], rs6.at[own]).start()
        else:
            out_remote()

    finish_kv(2)

    for n in range(8):
        landed(gwb.at[n], rs6.at[n])
        gw_out[:, n * GW : (n + 1) * GW] = gwb[n].astype(F32)

    def collect(hh, carry):
        for d in (1, 2, 3):
            ys = (y + 4 - d) % 4
            landed(back_slot(gq_out, hh, y, ys), rs7.at[hh * 3 + d - 1])
            for t in range(2):
                landed(back_slot((gk_out, gv_out)[t], hh, y, ys), rs9.at[(hh * 2 + t) * 3 + d - 1])
        landed(back_slot(gq_out, hh, y, y), ls7.at[hh])
        for t in range(2):
            landed(back_slot((gk_out, gv_out)[t], hh, y, y), ls9.at[hh * 2 + t])
        return carry

    lax.fori_loop(0, 3, collect, 0)

    @pl.when(z == y)
    def _():
        for n in range(3):
            landed(w_hbm, ssw1.at[n])

    for n in range(3):
        landed(w_own, ssw2.at[n])

    def left_head(hh, carry):
        for t in range(3):
            for d in (1, 2, 3):
                landed(slot(t, hh, y), ss1.at[(hh * 3 + t) * 3 + d - 1])
        for t in range(2):
            i = hh * 2 + t
            landed(kv_half(t, hh, xh), ss2.at[i])
            landed(pk.at[i], ss8.at[i])
            for d in (1, 2, 3):
                landed(fin.at[i, 0:TOK, :], ss9.at[i * 3 + d - 1])
        for d in (1, 2, 3):
            landed(gqb.at[hh, 0:TOK, :], ss7.at[hh * 3 + d - 1])
        return carry

    lax.fori_loop(0, 3, left_head, 0)
    for n in range(6):
        landed(go_slot(y, 0), ss3.at[n])

    def left_term(i, carry):
        landed(rsb.at[i], ss5.at[i])
        return carry

    lax.fori_loop(1, 32, left_term, 0)

    @pl.when(z != y)
    def _():
        landed(redb, ss6.at[0])

    for n in range(1, 8):
        landed(redb, ss6.at[n])


def local(query_rows, key_rows, value_rows, grad_out, w_out):
    any_spec = pl.BlockSpec(memory_space=pl.ANY)
    dma = pltpu.SemaphoreType.DMA
    vm = pltpu.VMEM
    rows = jax.ShapeDtypeStruct((1, TOK, HW), BF16)
    return pl.pallas_call(
        kernel,
        out_shape=(rows, rows, rows, jax.ShapeDtypeStruct((96, D), F32)),
        in_specs=[any_spec] * 5,
        out_specs=(any_spec, any_spec, any_spec, pl.BlockSpec(memory_space=pltpu.VMEM)),
        scratch_shapes=[
            vm((3, HALF, HD), BF16),
            vm((3, SEQ, HD), BF16),
            vm((3, SEQ, HD), BF16),
            vm((3, HD, SEQ), BF16),
            vm((3, HD, SEQ), BF16),
            vm((HALF, D), BF16),
            vm((GW, D), BF16),
            vm((SEQ, TOK), F32),
            vm((12, SEQ, TOK), BF16),
            vm((4, GW, TOK), BF16),
            vm((GW, HALF), BF16),
            vm((12, HD, TOK), F32),
            vm((12, 8, TOK), F32),
            vm((SEQ, HD), F32),
            vm((SEQ, HD), F32),
            vm((8, GW, GW), BF16),
            vm((32, 96, GW), BF16),
            vm((96, GW), BF16),
            vm((8, 96, GW), BF16),
            vm((3, HALF, HD), BF16),
            vm((6, HALF, HD), BF16),
            vm((6, HALF, HD), BF16),
            vm((6, HALF, HD), F32),
            vm((6, HALF, HD), BF16),
            dma((27,)), dma((27,)), dma((9,)),
            dma((6,)), dma((6,)),
            dma((6,)), dma((6,)), dma((1,)),
            dma((3,)), dma((1,)), dma((3,)), dma((3,)),
            dma((32,)), dma((32,)),
            dma((8,)), dma((8,)),
            dma((9,)), dma((9,)), dma((3,)),
            dma((6,)), dma((6,)),
            dma((18,)), dma((18,)), dma((6,)),
        ],
        compiler_params=pltpu.CompilerParams(
            has_side_effects=True, vmem_limit_bytes=60 * 1024 * 1024
        ),
    )(query_rows, key_rows, value_rows, grad_out, w_out)


def solution(mesh):
    in_specs = (
        P("fsdp", "rows", None),
        P("fsdp", "rows", None),
        P("fsdp", "rows", None),
        P("fsdp", "rows", None),
        P("fsdp", None),
    )
    out_specs = (
        P("fsdp", "rows", None),
        P("fsdp", "rows", None),
        P("fsdp", "rows", None),
        P("fsdp", None),
    )
    return jax.shard_map(local, mesh=mesh, in_specs=in_specs, out_specs=out_specs, check_vma=False)
```

```python
import math

import jax
import jax.numpy as jnp
from jax import lax
from jax.experimental import pallas as pl
from jax.experimental.pallas import tpu as pltpu
from jax.sharding import PartitionSpec as P

F32 = jnp.float32
BF16 = jnp.bfloat16
MESH = pl.DeviceIdType.MESH
D = 3072
HW = 1536
HD = 128
TOK = 256
GW = 384
SEQ = 2048
HALF = 1024
KC = 256
NK = SEQ // KC
SCALE = 1.0 / math.sqrt(HD)
CST = SCALE * math.log2(math.e)


def m128(x):
    return pl.multiple_of(x, 128)


def m256(x):
    return pl.multiple_of(x, 256)


def local_copy(src, dst, sem):
    return pltpu.make_async_copy(src, dst, sem)


def remote(src, dst, send_sem, recv_sem, dev):
    return pltpu.make_async_remote_copy(
        src_ref=src, dst_ref=dst, send_sem=send_sem, recv_sem=recv_sem,
        device_id=dev, device_id_type=MESH,
    )


def landed(ref, sem):
    pltpu.make_async_copy(ref, ref, sem).wait()


def dot(a, b):
    return jnp.dot(a, b, preferred_element_type=F32)


def kernel(
    q_hbm, k_hbm, v_hbm, go_hbm, w_hbm,
    gq_out, gk_out, gv_out, gw_out,
    qbuf, kbuf, vbuf, ktb, vtb, go, wbuf, sbuf, pbuf, gat, att, obuf, linv,
    dkacc, dvacc, termb, rsb, part, pin, redb, gwb, gqb, pk, xbuf, keep, fin,
    ss1, rs1, ls1, ss2, rs2, ss3, rs3, lsg, ssw1, rsw1, ssw2, rsw2,
    ss5, rs5, ss6, rs6, ss7, rs7, ls7, ss8, rs8, ss9, rs9, ls9, ss10, rs10,
):
    f = lax.axis_index("fsdp")
    r = lax.axis_index("rows")
    z, xl, c = f // 4, (f // 2) % 2, f % 2
    y, xh = r // 2, r % 2
    j = f % 4

    def dev(z_, xl_, c_, y_, xh_):
        return (z_ * 4 + xl_ * 2 + c_, y_ * 2 + xh_)

    def ydev(y_):
        return dev(z, xl, c, y_, xh)

    partner = dev(z, xl, c, y, 1 - xh)
    ins = (k_hbm, v_hbm, q_hbm)

    def slot(t, hh, ys):
        if t == 2:
            return qbuf.at[hh, pl.ds(m256(ys * TOK), TOK), :]
        return (kbuf, vbuf)[t].at[hh, pl.ds(m256((xh * 4 + ys) * TOK), TOK), :]

    def cols(t, hh, yd):
        return ins[t].at[0, :, pl.ds(m128(yd * GW + hh * HD), HD)]

    def w_rows(n):
        return wbuf.at[pl.ds(pl.multiple_of(n * 96, 32), 96), :]

    w_own = w_rows(j)

    @pl.when(z == y)
    def _():
        local_copy(w_hbm, w_own, rsw1.at[0]).start()
        for dz in (1, 2, 3):
            remote(w_hbm, w_own, ssw1.at[dz - 1], rsw1.at[0], dev((z + dz) % 4, xl, c, y, xh)).start()

    def send_head(hh, carry):
        for t in range(3):
            for d in (1, 3, 2):
                yd = (y + d) % 4
                i = (hh * 3 + t) * 3 + d - 1
                remote(cols(t, hh, yd), slot(t, hh, y), ss1.at[i], rs1.at[i], ydev(yd)).start()
            local_copy(cols(t, hh, y), slot(t, hh, y), ls1.at[hh * 3 + t]).start()
        return carry

    lax.fori_loop(0, 3, send_head, 0)

    def go_slot(ys, h, n=1):
        return go.at[pl.ds(pl.multiple_of(ys * TOK + h * 128, 128), 128 * n), :]

    def go_src(h):
        return go_hbm.at[0, pl.ds(h * 128, 128), :]

    yr, yl = (y + 1) % 4, (y + 3) % 4
    yo = (y + 2) % 4
    remote(go_src(0), go_slot(y, 0), ss3.at[0], rs3.at[0], ydev(yr)).start()
    remote(go_src(1), go_slot(y, 1), ss3.at[2], rs3.at[2], ydev(yl)).start()
    remote(go_src(1), go_slot(y, 1), ss3.at[1], rs3.at[1], ydev(yr)).start()
    remote(go_src(0), go_slot(y, 0), ss3.at[3], rs3.at[3], ydev(yl)).start()
    local_copy(go_hbm.at[0], go_slot(y, 0, 2), lsg.at[0]).start()

    def kv_half(t, hh, h):
        return (kbuf, vbuf)[t].at[hh, pl.ds(m256(h * HALF), HALF), :]

    def relay(hh, carry):
        for t in range(2):
            local_copy(cols(t, hh, y), slot(t, hh, y), ls1.at[hh * 3 + t]).wait()
            for d in (1, 3, 2):
                i = (hh * 3 + t) * 3 + d - 1
                landed(slot(t, hh, (y + 4 - d) % 4), rs1.at[i])
            i = hh * 2 + t
            half = kv_half(t, hh, xh)
            remote(half, half, ss2.at[i], rs2.at[i], partner).start()
        return carry

    lax.fori_loop(0, 3, relay, 0)

    landed(w_own, rsw1.at[0])
    remote(w_own, w_own, ssw2.at[0], rsw2.at[0], dev(z, xl, 1 - c, y, xh)).start()
    remote(w_own, w_own, ssw2.at[1], rsw2.at[1], dev(z, 1 - xl, c, y, xh)).start()

    def forward(hh, carry):
        for t in range(2):
            landed(kv_half(t, hh, 1 - xh), rs2.at[hh * 2 + t])
        local_copy(cols(2, hh, y), slot(2, hh, y), ls1.at[hh * 3 + 2]).wait()
        for d in (1, 3, 2):
            landed(slot(2, hh, (y + 4 - d) % 4), rs1.at[(hh * 3 + 2) * 3 + d - 1])
        for kc in range(NK):
            ks = slice(kc * KC, (kc + 1) * KC)
            ktb[hh, :, ks] = kbuf[hh, ks, :].T
            vtb[hh, :, ks] = vbuf[hh, ks, :].T

        def block(qb, carry):
            i = hh * 4 + qb
            qs = pl.ds(m256(qb * TOK), TOK)
            qt = qbuf[hh, qs, :].T
            m = jnp.full((1, TOK), -jnp.inf, F32)
            for kc in range(NK):
                ks = slice(kc * KC, (kc + 1) * KC)
                s = dot(kbuf[hh, ks, :], qt)
                sbuf[ks, :] = s
                m = jnp.maximum(m, jnp.max(s, axis=0, keepdims=True))
            mc = m * CST
            l = jnp.zeros((1, TOK), F32)
            o = jnp.zeros((HD, TOK), F32)
            for kc in range(NK):
                ks = slice(kc * KC, (kc + 1) * KC)
                p = jnp.exp2(sbuf[ks, :] * CST - mc)
                l = l + jnp.sum(p, axis=0, keepdims=True)
                pb = p.astype(BF16)
                pbuf[i, ks, :] = pb
                o = o + dot(vtb[hh, :, ks], pb)
            inv = 1.0 / l
            on = o * inv
            obuf[i] = on
            att[pl.ds(m128(hh * HD), HD), qs] = on.astype(BF16)
            linv[i] = jnp.broadcast_to(inv, (8, TOK))
            return carry

        return lax.fori_loop(0, 4, block, carry)

    forward(0, 0)
    w_across = w_rows((1 - xl) * 2 + c)
    landed(w_across, rsw2.at[1])
    remote(w_across, w_across, ssw2.at[2], rsw2.at[2], dev(z, xl, 1 - c, y, xh)).start()

    landed(go_slot(yl, 0), rs3.at[0])
    remote(go_slot(yl, 0), go_slot(yl, 0), ss3.at[4], rs3.at[4], ydev(yr)).start()
    landed(go_slot(yr, 1), rs3.at[2])
    remote(go_slot(yr, 1), go_slot(yr, 1), ss3.at[5], rs3.at[5], ydev(yl)).start()

    lax.fori_loop(1, 3, forward, 0)

    landed(w_rows(xl * 2 + 1 - c), rsw2.at[0])
    landed(w_rows((1 - xl) * 2 + 1 - c), rsw2.at[2])

    def project(ys):
        rows = pl.ds(m256(ys * TOK), TOK)
        g = lax.dot_general(wbuf[...], go[rows, :], (((1,), (1,)), ((), ())), preferred_element_type=F32)
        gat[ys] = g.astype(BF16)

    local_copy(go_hbm.at[0], go_slot(y, 0, 2), lsg.at[0]).wait()
    landed(go_slot(yl, 1), rs3.at[1])
    landed(go_slot(yr, 0), rs3.at[3])
    landed(go_slot(yo, 0), rs3.at[4])
    landed(go_slot(yo, 1), rs3.at[5])

    def project_all(d, carry):
        project((y + d) % 4)
        return carry

    lax.fori_loop(0, 4, project_all, 0)

    def term(o, carry):
        zd = (z + 1 + o) % 4
        for xd in range(2):
            cs = pl.ds(m128((zd * 2 + xd) * GW), GW)
            t = dot(att[...], go[:, cs]).astype(BF16)
            for n in range(4):
                termb[zd, n % 2, xd, n // 2] = t[n * 96 : (n + 1) * 96, :]
        for b in range(2):
            i = o * 2 + b
            cd = (c + b) % 2

            def go_out():
                remote(termb.at[zd, cd], rsb.at[i], ss5.at[i], rs5.at[i], dev(zd, xl, cd, y, xh)).start()

            if b == 0:
                pl.when(o < 3)(go_out)
            else:
                go_out()
        return carry

    lax.fori_loop(0, 4, term, 0)

    def reduce_planes():
        def add(i, carry):
            landed(rsb.at[i], rs5.at[i])
            return carry

        lax.fori_loop(0, 6, add, 0)
        landed(rsb.at[7], rs5.at[7])
        for e in range(2):
            for a in range(2):
                t = termb[z, c, e, a].astype(F32) + rsb[7, e, a].astype(F32)
                for i in range(6):
                    t = t + rsb[i, e, a].astype(F32)
                part[e, a] = t.astype(BF16)
        for n in (1, 2, 3):
            a, e = n // 2, n % 2
            xld, xhd = (xl + a) % 2, (xh + e) % 2
            remote(part.at[xhd, xld], pin.at[n], ss10.at[n], rs10.at[n], dev(z, xld, c, y, xhd)).start()

    def back_slot(out, hh, yd, ysrc):
        del yd
        return out.at[0, :, pl.ds(m128(ysrc * GW + hh * HD), HD)]

    def hand_out(buf, out, hh, ss, rs, ls, base, lbase):
        for d in (1, 3, 2):
            yd = (y + d) % 4
            remote(buf(yd), back_slot(out, hh, yd, y), ss.at[base + d - 1], rs.at[base + d - 1], ydev(yd)).start()
        local_copy(buf(y), back_slot(out, hh, y, y), ls.at[lbase]).start()

    def finish_kv(hh):
        for t in range(2):
            i = hh * 2 + t
            landed(xbuf.at[i], rs8.at[i])
            fin[i] = (keep[i] + xbuf[i].astype(F32)).astype(BF16)
            hand_out(
                lambda yd: fin.at[i, pl.ds(m256(yd * TOK), TOK), :],
                (gk_out, gv_out)[t], hh, ss9, rs9, ls9, i * 3, i,
            )

    def backward(hh, carry):
        dkacc[...] = jnp.zeros_like(dkacc)
        dvacc[...] = jnp.zeros_like(dvacc)

        def block(qb, carry):
            i = hh * 4 + qb
            qs = pl.ds(m256(qb * TOK), TOK)
            qn = qbuf[hh, qs, :]
            inv = linv[i][0:1, :]
            gt = (gat[qb, pl.ds(m128(hh * HD), HD), :].astype(F32) * inv).astype(BF16)
            gn = gt.T
            cen = jnp.sum(gt.astype(F32) * obuf[i], axis=0, keepdims=True)
            dq = jnp.zeros((HD, TOK), F32)
            for kc in range(NK):
                ks = slice(kc * KC, (kc + 1) * KC)
                dp = dot(vbuf[hh, ks, :], gt)
                pb = pbuf[i, ks, :]
                ds = (pb.astype(F32) * (dp - cen)).astype(BF16)
                dq = dq + dot(ktb[hh, :, ks], ds)
                dkacc[ks, :] += dot(ds, qn)
                dvacc[ks, :] += dot(pb, gn)
            gqb[hh, qs, :] = (dq * SCALE).T.astype(BF16)
            return carry

        lax.fori_loop(0, 4, block, 0)
        mine, other = pl.ds(m256(xh * HALF), HALF), pl.ds(m256((1 - xh) * HALF), HALF)
        for t in range(2):
            acc = (dkacc, dvacc)[t]
            fac = (SCALE, 1.0)[t]
            i = hh * 2 + t
            pk[i] = (acc[other, :] * fac).astype(BF16)
            remote(pk.at[i], xbuf.at[i], ss8.at[i], rs8.at[i], partner).start()
            keep[i] = acc[mine, :] * fac
        hand_out(lambda yd: gqb.at[hh, pl.ds(m256(yd * TOK), TOK), :], gq_out, hh, ss7, rs7, ls7, hh * 3, hh)

        @pl.when(hh > 0)
        def _():
            finish_kv(hh - 1)

        @pl.when(hh == 2)
        def _():
            reduce_planes()

        return carry

    lax.fori_loop(0, 3, backward, 0)

    own = z * 2 + xh
    acc = part[xh, xl].astype(F32)
    for n in (1, 2, 3):
        landed(pin.at[n], rs10.at[n])
        acc = acc + pin[n].astype(F32)
    redb[...] = acc.astype(BF16)
    for n in range(8):
        d, e = n // 2, n % 2
        yd, xd = (y + d) % 4, (xh + e) % 2

        def out_remote():
            remote(redb, gwb.at[own], ss6.at[n], rs6.at[own], dev(y, xl, c, yd, xd)).start()

        if n == 0:
            pl.when(z != y)(out_remote)

            @pl.when(z == y)
            def _():
                local_copy(redb, gwb.at[own], rs6.at[own]).start()
        else:
            out_remote()

    finish_kv(2)

    for n in range(8):
        landed(gwb.at[n], rs6.at[n])
        gw_out[:, n * GW : (n + 1) * GW] = gwb[n].astype(F32)

    def collect(hh, carry):
        for d in (1, 2, 3):
            ys = (y + 4 - d) % 4
            landed(back_slot(gq_out, hh, y, ys), rs7.at[hh * 3 + d - 1])
            for t in range(2):
                landed(back_slot((gk_out, gv_out)[t], hh, y, ys), rs9.at[(hh * 2 + t) * 3 + d - 1])
        landed(back_slot(gq_out, hh, y, y), ls7.at[hh])
        for t in range(2):
            landed(back_slot((gk_out, gv_out)[t], hh, y, y), ls9.at[hh * 2 + t])
        return carry

    lax.fori_loop(0, 3, collect, 0)

    @pl.when(z == y)
    def _():
        for n in range(3):
            landed(w_hbm, ssw1.at[n])

    for n in range(3):
        landed(w_own, ssw2.at[n])

    def left_head(hh, carry):
        for t in range(3):
            for d in (1, 2, 3):
                landed(slot(t, hh, y), ss1.at[(hh * 3 + t) * 3 + d - 1])
        for t in range(2):
            i = hh * 2 + t
            landed(kv_half(t, hh, xh), ss2.at[i])
            landed(pk.at[i], ss8.at[i])
            for d in (1, 2, 3):
                landed(fin.at[i, 0:TOK, :], ss9.at[i * 3 + d - 1])
        for d in (1, 2, 3):
            landed(gqb.at[hh, 0:TOK, :], ss7.at[hh * 3 + d - 1])
        return carry

    lax.fori_loop(0, 3, left_head, 0)
    for n in range(6):
        landed(go_slot(y, 0), ss3.at[n])

    for n in (0, 1, 2, 3, 4, 5, 7):
        landed(rsb.at[n], ss5.at[n])
    for n in (1, 2, 3):
        landed(redb, ss10.at[n])

    @pl.when(z != y)
    def _():
        landed(redb, ss6.at[0])

    for n in range(1, 8):
        landed(redb, ss6.at[n])


def local(query_rows, key_rows, value_rows, grad_out, w_out):
    any_spec = pl.BlockSpec(memory_space=pl.ANY)
    dma = pltpu.SemaphoreType.DMA
    vm = pltpu.VMEM
    rows = jax.ShapeDtypeStruct((1, TOK, HW), BF16)
    return pl.pallas_call(
        kernel,
        out_shape=(rows, rows, rows, jax.ShapeDtypeStruct((96, D), F32)),
        in_specs=[any_spec] * 5,
        out_specs=(any_spec, any_spec, any_spec, pl.BlockSpec(memory_space=pltpu.VMEM)),
        scratch_shapes=[
            vm((3, HALF, HD), BF16),
            vm((3, SEQ, HD), BF16),
            vm((3, SEQ, HD), BF16),
            vm((3, HD, SEQ), BF16),
            vm((3, HD, SEQ), BF16),
            vm((HALF, D), BF16),
            vm((GW, D), BF16),
            vm((SEQ, TOK), F32),
            vm((12, SEQ, TOK), BF16),
            vm((4, GW, TOK), BF16),
            vm((GW, HALF), BF16),
            vm((12, HD, TOK), F32),
            vm((12, 8, TOK), F32),
            vm((SEQ, HD), F32),
            vm((SEQ, HD), F32),
            vm((4, 2, 2, 2, 96, GW), BF16),
            vm((8, 2, 2, 96, GW), BF16),
            vm((2, 2, 96, GW), BF16),
            vm((4, 96, GW), BF16),
            vm((96, GW), BF16),
            vm((8, 96, GW), BF16),
            vm((3, HALF, HD), BF16),
            vm((6, HALF, HD), BF16),
            vm((6, HALF, HD), BF16),
            vm((6, HALF, HD), F32),
            vm((6, HALF, HD), BF16),
            dma((27,)), dma((27,)), dma((9,)),
            dma((6,)), dma((6,)),
            dma((6,)), dma((6,)), dma((1,)),
            dma((3,)), dma((1,)), dma((3,)), dma((3,)),
            dma((8,)), dma((8,)),
            dma((8,)), dma((8,)),
            dma((9,)), dma((9,)), dma((3,)),
            dma((6,)), dma((6,)),
            dma((18,)), dma((18,)), dma((6,)),
            dma((4,)), dma((4,)),
        ],
        compiler_params=pltpu.CompilerParams(
            has_side_effects=True, vmem_limit_bytes=60 * 1024 * 1024
        ),
    )(query_rows, key_rows, value_rows, grad_out, w_out)


def solution(mesh):
    in_specs = (
        P("fsdp", "rows", None),
        P("fsdp", "rows", None),
        P("fsdp", "rows", None),
        P("fsdp", "rows", None),
        P("fsdp", None),
    )
    out_specs = (
        P("fsdp", "rows", None),
        P("fsdp", "rows", None),
        P("fsdp", "rows", None),
        P("fsdp", None),
    )
    return jax.shard_map(local, mesh=mesh, in_specs=in_specs, out_specs=out_specs, check_vma=False)
```

```python
import math

import jax
import jax.numpy as jnp
from jax import lax
from jax.experimental import pallas as pl
from jax.experimental.pallas import tpu as pltpu
from jax.sharding import PartitionSpec as P

F32 = jnp.float32
BF16 = jnp.bfloat16
MESH = pl.DeviceIdType.MESH
D = 3072
HW = 1536
HD = 128
TOK = 256
GW = 384
HALF = 1024
KC = 256
NK = HALF // KC
SCALE = 1.0 / math.sqrt(HD)
CST = SCALE * math.log2(math.e)


def m128(x):
    return pl.multiple_of(x, 128)


def m256(x):
    return pl.multiple_of(x, 256)


def local_copy(src, dst, sem):
    return pltpu.make_async_copy(src, dst, sem)


def remote(src, dst, send_sem, recv_sem, dev):
    return pltpu.make_async_remote_copy(
        src_ref=src, dst_ref=dst, send_sem=send_sem, recv_sem=recv_sem,
        device_id=dev, device_id_type=MESH,
    )


def landed(ref, sem):
    pltpu.make_async_copy(ref, ref, sem).wait()


def dot(a, b):
    return jnp.dot(a, b, preferred_element_type=F32)


def kernel(
    q_hbm, k_hbm, v_hbm, go_hbm, w_hbm,
    gq_out, gk_out, gv_out, gw_out,
    qbuf, kbuf, vbuf, ktb, vtb, go, wbuf, sbuf, pbuf, att, obuf, stat, rbuf,
    oxs, oxr, sxs, sxr, g1, c1, gxs, gxr, cxs, cxr, dqk, dqxs, dqxr, finq,
    dkacc, dvacc, fin, termb, cin, zsum, zin, part, pin, redb, gwb,
    ss1, rs1, ls1, ss2, rs2, ss3, rs3, lsg, ssw1, rsw1, ssw2, rsw2,
    ss4, rs4, ss5, rs5, ss6, rs6, ss7, rs7, ls7, ss8, rs8, ss9, rs9, ls9,
    ss10, rs10, ss11, rs11, ss12, rs12,
):
    f = lax.axis_index("fsdp")
    r = lax.axis_index("rows")
    z, xl, c = f // 4, (f // 2) % 2, f % 2
    y, xh = r // 2, r % 2
    j = f % 4

    def dev(z_, xl_, c_, y_, xh_):
        return (z_ * 4 + xl_ * 2 + c_, y_ * 2 + xh_)

    def ydev(y_):
        return dev(z, xl, c, y_, xh)

    partner = dev(z, xl, c, y, 1 - xh)
    coremate = dev(z, xl, 1 - c, y, xh)
    ins = (k_hbm, v_hbm, q_hbm)

    def slot(t, hh, ys):
        if t == 2:
            return qbuf.at[hh, pl.ds(m256((xh * 4 + ys) * TOK), TOK), :]
        return (kbuf, vbuf)[t].at[hh, pl.ds(m256(ys * TOK), TOK), :]

    def cols(t, hh, yd):
        return ins[t].at[0, :, pl.ds(m128(yd * GW + hh * HD), HD)]

    def w_rows(n):
        return wbuf.at[pl.ds(pl.multiple_of(n * 96, 32), 96), :]

    w_own = w_rows(j)

    @pl.when(z == y)
    def _():
        local_copy(w_hbm, w_own, rsw1.at[0]).start()
        for dz in (1, 2, 3):
            remote(w_hbm, w_own, ssw1.at[dz - 1], rsw1.at[0], dev((z + dz) % 4, xl, c, y, xh)).start()

    def send_head(hh, carry):
        for t in (2, 0, 1):
            for d in (1, 3, 2):
                yd = (y + d) % 4
                i = (hh * 3 + t) * 3 + d - 1
                remote(cols(t, hh, yd), slot(t, hh, y), ss1.at[i], rs1.at[i], ydev(yd)).start()
            local_copy(cols(t, hh, y), slot(t, hh, y), ls1.at[hh * 3 + t]).start()
        return carry

    lax.fori_loop(0, 3, send_head, 0)

    def go_slot(ys, h, n=1):
        return go.at[pl.ds(pl.multiple_of(ys * TOK + h * 128, 128), 128 * n), :]

    def go_src(h):
        return go_hbm.at[0, pl.ds(h * 128, 128), :]

    yr, yl = (y + 1) % 4, (y + 3) % 4
    yo = (y + 2) % 4
    remote(go_src(0), go_slot(y, 0), ss3.at[0], rs3.at[0], ydev(yr)).start()
    remote(go_src(1), go_slot(y, 1), ss3.at[2], rs3.at[2], ydev(yl)).start()
    remote(go_src(1), go_slot(y, 1), ss3.at[1], rs3.at[1], ydev(yr)).start()
    remote(go_src(0), go_slot(y, 0), ss3.at[3], rs3.at[3], ydev(yl)).start()
    local_copy(go_hbm.at[0], go_slot(y, 0, 2), lsg.at[0]).start()

    def arrived(t, hh):
        local_copy(cols(t, hh, y), slot(t, hh, y), ls1.at[hh * 3 + t]).wait()
        for d in (1, 3, 2):
            landed(slot(t, hh, (y + 4 - d) % 4), rs1.at[(hh * 3 + t) * 3 + d - 1])

    def q_half(hh, h):
        return qbuf.at[hh, pl.ds(pl.multiple_of(h * HALF, HALF), HALF), :]

    def relay(hh, carry):
        arrived(2, hh)
        remote(q_half(hh, xh), q_half(hh, xh), ss2.at[hh], rs2.at[hh], partner).start()
        return carry

    lax.fori_loop(0, 3, relay, 0)

    landed(w_own, rsw1.at[0])
    remote(w_own, w_own, ssw2.at[0], rsw2.at[0], coremate).start()
    remote(w_own, w_own, ssw2.at[1], rsw2.at[1], dev(z, 1 - xl, c, y, xh)).start()

    def scores_block(hh, s):
        i = hh * 8 + s
        qt = qbuf[hh, pl.ds(m256(s * TOK), TOK), :].T
        m = jnp.full((1, TOK), -jnp.inf, F32)
        for kc in range(NK):
            ks = slice(kc * KC, (kc + 1) * KC)
            sc = dot(kbuf[hh, ks, :], qt)
            sbuf[ks, :] = sc
            m = jnp.maximum(m, jnp.max(sc, axis=0, keepdims=True))
        mc = m * CST
        l = jnp.zeros((1, TOK), F32)
        o = jnp.zeros((HD, TOK), F32)
        for kc in range(NK):
            ks = slice(kc * KC, (kc + 1) * KC)
            p = jnp.exp2(sbuf[ks, :] * CST - mc)
            l = l + jnp.sum(p, axis=0, keepdims=True)
            pb = p.astype(BF16)
            pbuf[i, ks, :] = pb
            o = o + dot(vtb[hh, :, ks], pb)
        return m, l, o

    def forward(hh, carry):
        arrived(0, hh)
        arrived(1, hh)
        for kc in range(NK):
            ks = slice(kc * KC, (kc + 1) * KC)
            ktb[hh, :, ks] = kbuf[hh, ks, :].T
            vtb[hh, :, ks] = vbuf[hh, ks, :].T
        landed(q_half(hh, 1 - xh), rs2.at[hh])

        def theirs(ys, carry):
            m, l, o = scores_block(hh, (1 - xh) * 4 + ys)
            oxs[hh, ys] = o.astype(BF16)
            sxs[hh, ys, 0:1, :] = m
            sxs[hh, ys, 1:2, :] = l
            return carry

        lax.fori_loop(0, 4, theirs, 0)
        remote(oxs.at[hh], oxr.at[hh], ss4.at[hh], rs4.at[hh], partner).start()
        remote(sxs.at[hh], sxr.at[hh], ss4.at[hh + 3], rs4.at[hh + 3], partner).start()

        def mine(ys, carry):
            m, l, o = scores_block(hh, xh * 4 + ys)
            obuf[hh, ys] = o
            stat[hh, ys, 0:1, :] = m
            stat[hh, ys, 1:2, :] = l
            return carry

        return lax.fori_loop(0, 4, mine, carry)

    lax.fori_loop(0, 3, forward, 0)

    w_across = w_rows((1 - xl) * 2 + c)
    landed(w_across, rsw2.at[1])
    remote(w_across, w_across, ssw2.at[2], rsw2.at[2], coremate).start()

    def merge(hh, carry):
        landed(oxr.at[hh], rs4.at[hh])
        landed(sxr.at[hh], rs4.at[hh + 3])

        def block(ys, carry):
            ma, la = stat[hh, ys, 0:1, :], stat[hh, ys, 1:2, :]
            mb, lb = sxr[hh, ys, 0:1, :], sxr[hh, ys, 1:2, :]
            m = jnp.maximum(ma, mb)
            ea, eb = jnp.exp2((ma - m) * CST), jnp.exp2((mb - m) * CST)
            inv = 1.0 / (la * ea + lb * eb)
            ra, rb = ea * inv, eb * inv
            o = obuf[hh, ys] * ra + oxr[hh, ys].astype(F32) * rb
            obuf[hh, ys] = o
            att[pl.ds(m128(hh * HD), HD), pl.ds(m256(ys * TOK), TOK)] = o.astype(BF16)
            rbuf[hh, ys, 0:1, :] = ra
            rbuf[hh, ys, 1:2, :] = rb
            return carry

        return lax.fori_loop(0, 4, block, carry)

    lax.fori_loop(0, 3, merge, 0)
    landed(w_rows(xl * 2 + 1 - c), rsw2.at[0])
    landed(w_rows((1 - xl) * 2 + 1 - c), rsw2.at[2])

    def project(ys):
        g = lax.dot_general(
            wbuf[...], go[pl.ds(m256(ys * TOK), TOK), :], (((1,), (1,)), ((), ())), preferred_element_type=F32
        )
        for hh in range(3):
            gh = g[hh * HD : (hh + 1) * HD, :]
            cen = jnp.sum(gh * obuf[hh, ys], axis=0, keepdims=True)
            ra, rb = rbuf[hh, ys, 0:1, :], rbuf[hh, ys, 1:2, :]
            g1[ys, hh] = (gh * ra).astype(BF16)
            gxs[ys, hh] = (gh * rb).astype(BF16)
            c1[ys, hh, 0:1, :] = cen * ra
            cxs[ys, hh, 0:1, :] = cen * rb
        remote(gxs.at[ys], gxr.at[ys], ss8.at[ys], rs8.at[ys], partner).start()
        remote(cxs.at[ys], cxr.at[ys], ss8.at[ys + 4], rs8.at[ys + 4], partner).start()

    dkacc[...] = jnp.zeros_like(dkacc)
    dvacc[...] = jnp.zeros_like(dvacc)

    def backward(own, ys, after=None):
        s = (xh if own else 1 - xh) * 4 + ys

        def head(hh, carry):
            i = hh * 8 + s
            qn = qbuf[hh, pl.ds(m256(s * TOK), TOK), :]
            gt = (g1 if own else gxr)[ys, hh]
            cen = (c1 if own else cxr)[ys, hh, 0:1, :]
            gn = gt.T
            dq = jnp.zeros((HD, TOK), F32)
            for kc in range(NK):
                ks = slice(kc * KC, (kc + 1) * KC)
                dp = dot(vbuf[hh, ks, :], gt)
                pb = pbuf[i, ks, :]
                ds = (pb.astype(F32) * (dp - cen)).astype(BF16)
                dq = dq + dot(ktb[hh, :, ks], ds)
                dkacc[hh, ks, :] += dot(ds, qn)
                dvacc[hh, ks, :] += dot(pb, gn)
            dqn = (dq * SCALE).T
            hs = pl.ds(m128(hh * HD), HD)
            if own:
                dqk[ys, :, hs] = dqn
            else:
                dqxs[ys, :, hs] = dqn.astype(BF16)
            if after is not None:
                after(hh)
            return carry

        lax.fori_loop(0, 3, head, 0)

    def theirs_in(ys):
        landed(gxr.at[ys], rs8.at[ys])
        landed(cxr.at[ys], rs8.at[ys + 4])

    def send_dq(ys):
        remote(dqxs.at[ys], dqxr.at[ys], ss12.at[ys], rs12.at[ys], partner).start()

    def q_cols(ysrc):
        return gq_out.at[0, :, pl.ds(m128(ysrc * GW), GW)]

    def finish_q(d):
        ys = (y + d) % 4
        landed(dqxr.at[ys], rs12.at[ys])
        finq[ys] = (dqk[ys] + dqxr[ys].astype(F32)).astype(BF16)
        if d == 0:
            local_copy(finq.at[ys], q_cols(y), ls7.at[0]).start()
        else:
            remote(finq.at[ys], q_cols(y), ss7.at[d - 1], rs7.at[d - 1], ydev(ys)).start()

    local_copy(go_hbm.at[0], go_slot(y, 0, 2), lsg.at[0]).wait()
    project(y)
    backward(True, y)

    landed(go_slot(yl, 0), rs3.at[0])
    remote(go_slot(yl, 0), go_slot(yl, 0), ss3.at[4], rs3.at[4], ydev(yr)).start()
    landed(go_slot(yr, 1), rs3.at[2])
    remote(go_slot(yr, 1), go_slot(yr, 1), ss3.at[5], rs3.at[5], ydev(yl)).start()

    theirs_in(y)
    backward(False, y)
    send_dq(y)

    landed(go_slot(yl, 1), rs3.at[1])
    project(yl)
    finish_q(0)
    backward(True, yl)
    landed(go_slot(yr, 0), rs3.at[3])
    project(yr)
    theirs_in(yl)
    backward(False, yl)
    send_dq(yl)
    backward(True, yr)
    theirs_in(yr)
    backward(False, yr)
    send_dq(yr)
    finish_q(3)

    landed(go_slot(yo, 0), rs3.at[4])
    landed(go_slot(yo, 1), rs3.at[5])
    project(yo)

    def term(o, carry):
        zd = (z + 1 + o) % 4
        for xd in range(2):
            cs = pl.ds(m128((zd * 2 + xd) * GW), GW)
            t = dot(att[...], go[:, cs]).astype(BF16)
            for n in range(4):
                termb[zd, n % 2, xd, n // 2] = t[n * 96 : (n + 1) * 96, :]
        remote(termb.at[zd, 1 - c], cin.at[zd], ss5.at[zd], rs5.at[zd], coremate).start()
        return carry

    lax.fori_loop(0, 4, term, 0)
    backward(True, yo)

    def to_z(o, carry):
        zd = (z + 1 + o) % 4
        landed(cin.at[zd], rs5.at[zd])
        for e in range(2):
            for a in range(2):
                t = termb[zd, c, e, a].astype(F32) + cin[zd, e, a].astype(F32)
                zsum[o, e, a] = t.astype(BF16)

        @pl.when(o < 3)
        def _():
            remote(zsum.at[o], zin.at[o], ss11.at[o], rs11.at[o], dev(zd, xl, c, y, xh)).start()

        return carry

    lax.fori_loop(0, 4, to_z, 0)
    finish_q(1)

    def back_slot(out, hh, ysrc):
        return out.at[0, :, pl.ds(m128(ysrc * GW + hh * HD), HD)]

    def hand_out(hh):
        for t in range(2):
            i = hh * 2 + t
            fin[i] = ((dkacc, dvacc)[t][hh] * (SCALE, 1.0)[t]).astype(BF16)
            out = (gk_out, gv_out)[t]
            for d in (1, 3, 2):
                yd = (y + d) % 4
                n = i * 3 + d - 1
                remote(fin.at[i, pl.ds(m256(yd * TOK), TOK), :], back_slot(out, hh, y), ss9.at[n], rs9.at[n],
                       ydev(yd)).start()
            local_copy(fin.at[i, pl.ds(m256(y * TOK), TOK), :], back_slot(out, hh, y), ls9.at[i]).start()

    theirs_in(yo)
    backward(False, yo, hand_out)
    send_dq(yo)

    for i in range(3):
        landed(zin.at[i], rs11.at[i])
    for e in range(2):
        for a in range(2):
            t = zsum[3, e, a].astype(F32)
            for i in range(3):
                t = t + zin[i, e, a].astype(F32)
            part[e, a] = t.astype(BF16)
    for n in (1, 2, 3):
        a, e = n // 2, n % 2
        xld, xhd = (xl + a) % 2, (xh + e) % 2
        remote(part.at[xhd, xld], pin.at[n], ss10.at[n], rs10.at[n], dev(z, xld, c, y, xhd)).start()
    finish_q(2)

    own = z * 2 + xh
    acc = part[xh, xl].astype(F32)
    for n in (1, 2, 3):
        landed(pin.at[n], rs10.at[n])
        acc = acc + pin[n].astype(F32)
    redb[...] = acc.astype(BF16)
    for n in range(8):
        d, e = n // 2, n % 2
        yd, xd = (y + d) % 4, (xh + e) % 2

        def out_remote():
            remote(redb, gwb.at[own], ss6.at[n], rs6.at[own], dev(y, xl, c, yd, xd)).start()

        if n == 0:
            pl.when(z != y)(out_remote)

            @pl.when(z == y)
            def _():
                local_copy(redb, gwb.at[own], rs6.at[own]).start()
        else:
            out_remote()

    landed(q_cols(y), ls7.at[0])
    for d in (1, 2, 3):
        landed(q_cols((y + 4 - d) % 4), rs7.at[d - 1])

    def collect(hh, carry):
        for t in range(2):
            i = hh * 2 + t
            out = (gk_out, gv_out)[t]
            for d in (1, 2, 3):
                landed(back_slot(out, hh, (y + 4 - d) % 4), rs9.at[i * 3 + d - 1])
            landed(back_slot(out, hh, y), ls9.at[i])
        return carry

    lax.fori_loop(0, 3, collect, 0)
    for n in range(8):
        landed(gwb.at[n], rs6.at[n])
        gw_out[:, n * GW : (n + 1) * GW] = gwb[n].astype(F32)

    @pl.when(z == y)
    def _():
        for n in range(3):
            landed(w_hbm, ssw1.at[n])

    for n in range(3):
        landed(w_own, ssw2.at[n])

    def left_head(hh, carry):
        for t in range(3):
            for d in (1, 2, 3):
                landed(slot(t, hh, y), ss1.at[(hh * 3 + t) * 3 + d - 1])
        landed(q_half(hh, xh), ss2.at[hh])
        landed(oxs.at[hh], ss4.at[hh])
        landed(sxs.at[hh], ss4.at[hh + 3])
        for t in range(2):
            for d in (1, 2, 3):
                landed(fin.at[hh, 0:TOK, :], ss9.at[(hh * 2 + t) * 3 + d - 1])
        return carry

    lax.fori_loop(0, 3, left_head, 0)
    for n in range(6):
        landed(go_slot(y, 0), ss3.at[n])
    for n in range(4):
        landed(gxs.at[n], ss8.at[n])
        landed(cxs.at[n], ss8.at[n + 4])
        landed(dqxs.at[n], ss12.at[n])
        landed(cin.at[n], ss5.at[n])
    for n in range(3):
        landed(finq.at[n], ss7.at[n])
        landed(zin.at[n], ss11.at[n])
        landed(redb, ss10.at[n + 1])

    @pl.when(z != y)
    def _():
        landed(redb, ss6.at[0])

    for n in range(1, 8):
        landed(redb, ss6.at[n])


def local(query_rows, key_rows, value_rows, grad_out, w_out):
    any_spec = pl.BlockSpec(memory_space=pl.ANY)
    dma = pltpu.SemaphoreType.DMA
    vm = pltpu.VMEM
    rows = jax.ShapeDtypeStruct((1, TOK, HW), BF16)
    return pl.pallas_call(
        kernel,
        out_shape=(rows, rows, rows, jax.ShapeDtypeStruct((96, D), F32)),
        in_specs=[any_spec] * 5,
        out_specs=(any_spec, any_spec, any_spec, pl.BlockSpec(memory_space=pltpu.VMEM)),
        scratch_shapes=[
            vm((3, 2 * HALF, HD), BF16),
            vm((3, HALF, HD), BF16),
            vm((3, HALF, HD), BF16),
            vm((3, HD, HALF), BF16),
            vm((3, HD, HALF), BF16),
            vm((HALF, D), BF16),
            vm((GW, D), BF16),
            vm((HALF, TOK), F32),
            vm((24, HALF, TOK), BF16),
            vm((GW, HALF), BF16),
            vm((3, 4, HD, TOK), F32),
            vm((3, 4, 8, TOK), F32),
            vm((3, 4, 8, TOK), F32),
            vm((3, 4, HD, TOK), BF16),
            vm((3, 4, HD, TOK), BF16),
            vm((3, 4, 8, TOK), F32),
            vm((3, 4, 8, TOK), F32),
            vm((4, 3, HD, TOK), BF16),
            vm((4, 3, 8, TOK), F32),
            vm((4, 3, HD, TOK), BF16),
            vm((4, 3, HD, TOK), BF16),
            vm((4, 3, 8, TOK), F32),
            vm((4, 3, 8, TOK), F32),
            vm((4, TOK, GW), F32),
            vm((4, TOK, GW), BF16),
            vm((4, TOK, GW), BF16),
            vm((4, TOK, GW), BF16),
            vm((3, HALF, HD), F32),
            vm((3, HALF, HD), F32),
            vm((6, HALF, HD), BF16),
            vm((4, 2, 2, 2, 96, GW), BF16),
            vm((4, 2, 2, 96, GW), BF16),
            vm((4, 2, 2, 96, GW), BF16),
            vm((3, 2, 2, 96, GW), BF16),
            vm((2, 2, 96, GW), BF16),
            vm((4, 96, GW), BF16),
            vm((96, GW), BF16),
            vm((8, 96, GW), BF16),
            dma((27,)), dma((27,)), dma((9,)),
            dma((3,)), dma((3,)),
            dma((6,)), dma((6,)), dma((1,)),
            dma((3,)), dma((1,)), dma((3,)), dma((3,)),
            dma((6,)), dma((6,)),
            dma((4,)), dma((4,)),
            dma((8,)), dma((8,)),
            dma((3,)), dma((3,)), dma((1,)),
            dma((8,)), dma((8,)),
            dma((18,)), dma((18,)), dma((6,)),
            dma((4,)), dma((4,)),
            dma((3,)), dma((3,)),
            dma((4,)), dma((4,)),
        ],
        compiler_params=pltpu.CompilerParams(
            has_side_effects=True, vmem_limit_bytes=60 * 1024 * 1024
        ),
    )(query_rows, key_rows, value_rows, grad_out, w_out)


def solution(mesh):
    in_specs = (
        P("fsdp", "rows", None),
        P("fsdp", "rows", None),
        P("fsdp", "rows", None),
        P("fsdp", "rows", None),
        P("fsdp", None),
    )
    out_specs = (
        P("fsdp", "rows", None),
        P("fsdp", "rows", None),
        P("fsdp", "rows", None),
        P("fsdp", None),
    )
    return jax.shard_map(local, mesh=mesh, in_specs=in_specs, out_specs=out_specs, check_vma=False)
```

```python
import math

import jax
import jax.numpy as jnp
from jax import lax
from jax.experimental import pallas as pl
from jax.experimental.pallas import tpu as pltpu
from jax.sharding import PartitionSpec as P

F32 = jnp.float32
BF16 = jnp.bfloat16
MESH = pl.DeviceIdType.MESH
D = 3072
HW = 1536
HD = 128
TOK = 256
GW = 384
HALF = 1024
KC = 256
NK = HALF // KC
SCALE = 1.0 / math.sqrt(HD)
CST = SCALE * math.log2(math.e)


def m128(x):
    return pl.multiple_of(x, 128)


def m256(x):
    return pl.multiple_of(x, 256)


def local_copy(src, dst, sem):
    return pltpu.make_async_copy(src, dst, sem)


def remote(src, dst, send_sem, recv_sem, dev):
    return pltpu.make_async_remote_copy(
        src_ref=src, dst_ref=dst, send_sem=send_sem, recv_sem=recv_sem,
        device_id=dev, device_id_type=MESH,
    )


def landed(ref, sem):
    pltpu.make_async_copy(ref, ref, sem).wait()


def dot(a, b):
    return jnp.dot(a, b, preferred_element_type=F32)


def kernel(
    q_hbm, k_hbm, v_hbm, go_hbm, w_hbm,
    gq_out, gk_out, gv_out, gw_out,
    qbuf, kbuf, vbuf, ktb, vtb, go, wbuf, sbuf, pbuf, att, obuf, stat, rbuf,
    oxs, oxr, sxs, sxr, g1, c1, gxs, gxr, cxs, cxr, dqk, dqxs, dqxr, finq,
    dkacc, dvacc, fin, termb, cin, zsum, zin, part, pin, gst, tacc,
    ss1, rs1, ls1, ss2, rs2, ss3, rs3, lsg, ssw1, rsw1, ssw2, rsw2,
    ss4, rs4, ss5, rs5, ss6, rs6, ss7, rs7, ls7, ss8, rs8, ss9, rs9, ls9,
    ss10, rs10, ss11, rs11, ss12, rs12, ss13, rs13, lsw,
):
    f = lax.axis_index("fsdp")
    r = lax.axis_index("rows")
    z, xl, c = f // 4, (f // 2) % 2, f % 2
    y, xh = r // 2, r % 2
    j = f % 4

    def dev(z_, xl_, c_, y_, xh_):
        return (z_ * 4 + xl_ * 2 + c_, y_ * 2 + xh_)

    def ydev(y_):
        return dev(z, xl, c, y_, xh)

    partner = dev(z, xl, c, y, 1 - xh)
    coremate = dev(z, xl, 1 - c, y, xh)
    ins = (k_hbm, v_hbm, q_hbm)

    def slot(t, hh, ys):
        if t == 2:
            return qbuf.at[hh, pl.ds(m256((xh * 4 + ys) * TOK), TOK), :]
        return (kbuf, vbuf)[t].at[hh, pl.ds(m256(ys * TOK), TOK), :]

    def cols(t, hh, yd):
        return ins[t].at[0, :, pl.ds(m128(yd * GW + hh * HD), HD)]

    def w_rows(n):
        return wbuf.at[pl.ds(pl.multiple_of(n * 96, 32), 96), :]

    w_own = w_rows(j)

    barrier = pltpu.get_barrier_semaphore()

    def hello(d):
        pl.semaphore_signal(barrier, inc=1, device_id=d, device_id_type=MESH)

    for d in (1, 2, 3):
        hello(ydev((y + d) % 4))
        hello(dev(z, xl, c, (y + d) % 4, 1 - xh))
        hello(dev((z + d) % 4, xl, c, y, xh))
        hello(dev(z, (xl + d // 2) % 2, c, y, (xh + d % 2) % 2))
    hello(coremate)
    pl.semaphore_wait(barrier, 13)

    @pl.when(z == y)
    def _():
        local_copy(w_hbm, w_own, rsw1.at[0]).start()
        for dz in (1, 2, 3):
            remote(w_hbm, w_own, ssw1.at[dz - 1], rsw1.at[0], dev((z + dz) % 4, xl, c, y, xh)).start()

    def send_head(hh, carry):
        for t in (2, 0, 1):
            for d in (1, 3, 2):
                yd = (y + d) % 4
                i = (hh * 3 + t) * 3 + d - 1
                remote(cols(t, hh, yd), slot(t, hh, y), ss1.at[i], rs1.at[i], ydev(yd)).start()
            local_copy(cols(t, hh, y), slot(t, hh, y), ls1.at[hh * 3 + t]).start()
        return carry

    lax.fori_loop(0, 3, send_head, 0)

    def go_slot(ys, h, n=1):
        return go.at[pl.ds(pl.multiple_of(ys * TOK + h * 128, 128), 128 * n), :]

    def go_src(h):
        return go_hbm.at[0, pl.ds(h * 128, 128), :]

    yr, yl = (y + 1) % 4, (y + 3) % 4
    yo = (y + 2) % 4
    remote(go_src(0), go_slot(y, 0), ss3.at[0], rs3.at[0], ydev(yr)).start()
    remote(go_src(1), go_slot(y, 1), ss3.at[2], rs3.at[2], ydev(yl)).start()
    remote(go_src(1), go_slot(y, 1), ss3.at[1], rs3.at[1], ydev(yr)).start()
    remote(go_src(0), go_slot(y, 0), ss3.at[3], rs3.at[3], ydev(yl)).start()
    local_copy(go_hbm.at[0], go_slot(y, 0, 2), lsg.at[0]).start()

    def arrived(t, hh):
        local_copy(cols(t, hh, y), slot(t, hh, y), ls1.at[hh * 3 + t]).wait()
        for d in (1, 3, 2):
            landed(slot(t, hh, (y + 4 - d) % 4), rs1.at[(hh * 3 + t) * 3 + d - 1])

    def q_half(hh, h):
        return qbuf.at[hh, pl.ds(pl.multiple_of(h * HALF, HALF), HALF), :]

    def relay(hh, carry):
        arrived(2, hh)
        remote(q_half(hh, xh), q_half(hh, xh), ss2.at[hh], rs2.at[hh], partner).start()
        return carry

    lax.fori_loop(0, 3, relay, 0)

    landed(w_own, rsw1.at[0])
    remote(w_own, w_own, ssw2.at[0], rsw2.at[0], coremate).start()
    remote(w_own, w_own, ssw2.at[1], rsw2.at[1], dev(z, 1 - xl, c, y, xh)).start()

    def scores_block(hh, s):
        i = hh * 8 + s
        qt = qbuf[hh, pl.ds(m256(s * TOK), TOK), :].T
        m = jnp.full((1, TOK), -jnp.inf, F32)
        for kc in range(NK):
            ks = slice(kc * KC, (kc + 1) * KC)
            sc = dot(kbuf[hh, ks, :], qt)
            sbuf[ks, :] = sc
            m = jnp.maximum(m, jnp.max(sc, axis=0, keepdims=True))
        mc = m * CST
        l = jnp.zeros((1, TOK), F32)
        o = jnp.zeros((HD, TOK), F32)
        for kc in range(NK):
            ks = slice(kc * KC, (kc + 1) * KC)
            p = jnp.exp2(sbuf[ks, :] * CST - mc)
            l = l + jnp.sum(p, axis=0, keepdims=True)
            pb = p.astype(BF16)
            pbuf[i, ks, :] = pb
            o = o + dot(vtb[hh, :, ks], pb)
        return m, l, o

    def forward(hh, carry):
        arrived(0, hh)
        arrived(1, hh)
        for kc in range(NK):
            ks = slice(kc * KC, (kc + 1) * KC)
            ktb[hh, :, ks] = kbuf[hh, ks, :].T
            vtb[hh, :, ks] = vbuf[hh, ks, :].T
        landed(q_half(hh, 1 - xh), rs2.at[hh])

        def theirs(ys, carry):
            m, l, o = scores_block(hh, (1 - xh) * 4 + ys)
            oxs[hh, ys] = o.astype(BF16)
            sxs[hh, ys, 0:1, :] = m
            sxs[hh, ys, 1:2, :] = l
            return carry

        lax.fori_loop(0, 4, theirs, 0)
        remote(oxs.at[hh], oxr.at[hh], ss4.at[hh], rs4.at[hh], partner).start()
        remote(sxs.at[hh], sxr.at[hh], ss4.at[hh + 3], rs4.at[hh + 3], partner).start()

        def mine(ys, carry):
            m, l, o = scores_block(hh, xh * 4 + ys)
            obuf[hh, ys] = o
            stat[hh, ys, 0:1, :] = m
            stat[hh, ys, 1:2, :] = l
            return carry

        return lax.fori_loop(0, 4, mine, carry)

    lax.fori_loop(0, 3, forward, 0)

    w_across = w_rows((1 - xl) * 2 + c)
    landed(w_across, rsw2.at[1])
    remote(w_across, w_across, ssw2.at[2], rsw2.at[2], coremate).start()

    def merge(hh, carry):
        landed(oxr.at[hh], rs4.at[hh])
        landed(sxr.at[hh], rs4.at[hh + 3])

        def block(ys, carry):
            ma, la = stat[hh, ys, 0:1, :], stat[hh, ys, 1:2, :]
            mb, lb = sxr[hh, ys, 0:1, :], sxr[hh, ys, 1:2, :]
            m = jnp.maximum(ma, mb)
            ea, eb = jnp.exp2((ma - m) * CST), jnp.exp2((mb - m) * CST)
            inv = 1.0 / (la * ea + lb * eb)
            ra, rb = ea * inv, eb * inv
            o = obuf[hh, ys] * ra + oxr[hh, ys].astype(F32) * rb
            obuf[hh, ys] = o
            att[pl.ds(m128(hh * HD), HD), pl.ds(m256(ys * TOK), TOK)] = o.astype(BF16)
            rbuf[hh, ys, 0:1, :] = ra
            rbuf[hh, ys, 1:2, :] = rb
            return carry

        return lax.fori_loop(0, 4, block, carry)

    lax.fori_loop(0, 3, merge, 0)
    landed(w_rows(xl * 2 + 1 - c), rsw2.at[0])
    landed(w_rows((1 - xl) * 2 + 1 - c), rsw2.at[2])

    def project(ys):
        g = lax.dot_general(
            wbuf[...], go[pl.ds(m256(ys * TOK), TOK), :], (((1,), (1,)), ((), ())), preferred_element_type=F32
        )
        for hh in range(3):
            gh = g[hh * HD : (hh + 1) * HD, :]
            cen = jnp.sum(gh * obuf[hh, ys], axis=0, keepdims=True)
            ra, rb = rbuf[hh, ys, 0:1, :], rbuf[hh, ys, 1:2, :]
            g1[ys, hh] = (gh * ra).astype(BF16)
            gxs[ys, hh] = (gh * rb).astype(BF16)
            c1[ys, hh, 0:1, :] = cen * ra
            cxs[ys, hh, 0:1, :] = cen * rb
        remote(gxs.at[ys], gxr.at[ys], ss8.at[ys], rs8.at[ys], partner).start()
        remote(cxs.at[ys], cxr.at[ys], ss8.at[ys + 4], rs8.at[ys + 4], partner).start()

    dkacc[...] = jnp.zeros_like(dkacc)
    dvacc[...] = jnp.zeros_like(dvacc)

    def backward(own, ys, after=None):
        s = (xh if own else 1 - xh) * 4 + ys

        def head(hh, carry):
            i = hh * 8 + s
            qn = qbuf[hh, pl.ds(m256(s * TOK), TOK), :]
            gt = (g1 if own else gxr)[ys, hh]
            cen = (c1 if own else cxr)[ys, hh, 0:1, :]
            gn = gt.T
            dq = jnp.zeros((HD, TOK), F32)
            for kc in range(NK):
                ks = slice(kc * KC, (kc + 1) * KC)
                dp = dot(vbuf[hh, ks, :], gt)
                pb = pbuf[i, ks, :]
                ds = (pb.astype(F32) * (dp - cen)).astype(BF16)
                dq = dq + dot(ktb[hh, :, ks], ds)
                dkacc[hh, ks, :] += dot(ds, qn)
                dvacc[hh, ks, :] += dot(pb, gn)
            dqn = (dq * SCALE).T
            hs = pl.ds(m128(hh * HD), HD)
            if own:
                dqk[ys, :, hs] = dqn
            else:
                dqxs[ys, :, hs] = dqn.astype(BF16)
            if after is not None:
                after(hh)
            return carry

        lax.fori_loop(0, 3, head, 0)

    def theirs_in(ys):
        landed(gxr.at[ys], rs8.at[ys])
        landed(cxr.at[ys], rs8.at[ys + 4])

    def send_dq(ys):
        remote(dqxs.at[ys], dqxr.at[ys], ss12.at[ys], rs12.at[ys], partner).start()

    def q_cols(ysrc):
        return gq_out.at[0, :, pl.ds(m128(ysrc * GW), GW)]

    def finish_q(d):
        ys = (y + d) % 4
        landed(dqxr.at[ys], rs12.at[ys])
        finq[ys] = (dqk[ys] + dqxr[ys].astype(F32)).astype(BF16)
        if d == 0:
            local_copy(finq.at[ys], q_cols(y), ls7.at[0]).start()
        else:
            remote(finq.at[ys], q_cols(y), ss7.at[d - 1], rs7.at[d - 1], ydev(ys)).start()

    local_copy(go_hbm.at[0], go_slot(y, 0, 2), lsg.at[0]).wait()
    project(y)
    backward(True, y)

    landed(go_slot(yl, 0), rs3.at[0])
    remote(go_slot(yl, 0), go_slot(yl, 0), ss3.at[4], rs3.at[4], ydev(yr)).start()
    landed(go_slot(yr, 1), rs3.at[2])
    remote(go_slot(yr, 1), go_slot(yr, 1), ss3.at[5], rs3.at[5], ydev(yl)).start()

    theirs_in(y)
    backward(False, y)
    send_dq(y)

    def term_cols(zd, xd):
        return pl.ds(m128((zd * 2 + xd) * GW), GW)

    def term_dot(ys, zd, xd):
        at = pl.ds(m256(ys * TOK), TOK)
        return dot(att[:, at], go[at, term_cols(zd, xd)])

    def term_part(ys, first=False):
        def add(n, carry):
            t = term_dot(ys, n // 2, n % 2)
            tacc[n] = t if first else tacc[n] + t
            return carry

        lax.fori_loop(0, 8, add, 0)

    term_part(y, True)
    landed(go_slot(yl, 1), rs3.at[1])
    project(yl)
    backward(True, yl)
    landed(go_slot(yr, 0), rs3.at[3])
    project(yr)
    theirs_in(yl)
    backward(False, yl)
    send_dq(yl)
    backward(True, yr)
    theirs_in(yr)
    backward(False, yr)
    send_dq(yr)
    term_part(yl)
    term_part(yr)
    finish_q(0)

    landed(go_slot(yo, 0), rs3.at[4])
    landed(go_slot(yo, 1), rs3.at[5])
    project(yo)

    def term(o, carry):
        zd = (z + 1 + o) % 4
        for xd in range(2):
            t = (tacc[zd * 2 + xd] + term_dot(yo, zd, xd)).astype(BF16)
            for n in range(4):
                termb[zd, n % 2, xd, n // 2] = t[n * 96 : (n + 1) * 96, :]
        remote(termb.at[zd, 1 - c], cin.at[zd], ss5.at[zd], rs5.at[zd], coremate).start()
        return carry

    lax.fori_loop(0, 4, term, 0)
    finish_q(3)
    finish_q(1)
    backward(True, yo)

    def to_z(o, carry):
        zd = (z + 1 + o) % 4
        landed(cin.at[zd], rs5.at[zd])
        for e in range(2):
            for a in range(2):
                t = termb[zd, c, e, a].astype(F32) + cin[zd, e, a].astype(F32)
                zsum[o, e, a] = t.astype(BF16)

        @pl.when(o < 3)
        def _():
            remote(zsum.at[o], zin.at[o], ss11.at[o], rs11.at[o], dev(zd, xl, c, y, xh)).start()

        return carry

    lax.fori_loop(0, 4, to_z, 0)

    def back_slot(out, hh, ysrc):
        return out.at[0, :, pl.ds(m128(ysrc * GW + hh * HD), HD)]

    def hand_out(hh):
        for t in range(2):
            i = hh * 2 + t
            fin[i] = ((dkacc, dvacc)[t][hh] * (SCALE, 1.0)[t]).astype(BF16)
            out = (gk_out, gv_out)[t]
            for d in (1, 3, 2):
                yd = (y + d) % 4
                n = i * 3 + d - 1
                remote(fin.at[i, pl.ds(m256(yd * TOK), TOK), :], back_slot(out, hh, y), ss9.at[n], rs9.at[n],
                       ydev(yd)).start()
            local_copy(fin.at[i, pl.ds(m256(y * TOK), TOK), :], back_slot(out, hh, y), ls9.at[i]).start()

    theirs_in(yo)
    backward(False, yo, hand_out)
    send_dq(yo)

    for i in range(3):
        landed(zin.at[i], rs11.at[i])
    for e in range(2):
        for a in range(2):
            t = zsum[3, e, a].astype(F32)
            for i in range(3):
                t = t + zin[i, e, a].astype(F32)
            part[e, a] = t.astype(BF16)
    for n in (1, 2, 3):
        a, e = n // 2, n % 2
        xld, xhd = (xl + a) % 2, (xh + e) % 2
        remote(part.at[xhd, xld], pin.at[n], ss10.at[n], rs10.at[n], dev(z, xld, c, y, xhd)).start()
    finish_q(2)

    acc = part[xh, xl].astype(F32)
    for n in (1, 2, 3):
        landed(pin.at[n], rs10.at[n])
        acc = acc + pin[n].astype(F32)
    gst[y, xh] = acc.astype(BF16)
    for n in range(1, 8):
        d, e = n // 2, n % 2
        remote(gst.at[y, xh], gst.at[y, xh], ss6.at[n], rs6.at[n], dev(z, xl, c, (y + d) % 4, (xh + e) % 2)).start()
    for n in range(1, 8):
        d, e = n // 2, n % 2
        landed(gst.at[(y + 4 - d) % 4, (xh + e) % 2], rs6.at[n])

    def gw_cols(zs, e):
        return gw_out.at[:, pl.ds(m128((zs * 2 + e) * GW), GW)]

    for d in (1, 2, 3):
        zd = (z + d) % 4
        for e in range(2):
            n = (d - 1) * 2 + e
            remote(gst.at[zd, e], gw_cols(z, e), ss13.at[n], rs13.at[n], dev(zd, xl, c, y, xh)).start()
    for e in range(2):
        local_copy(gst.at[z, e], gw_cols(z, e), lsw.at[e]).start()

    landed(q_cols(y), ls7.at[0])
    for d in (1, 2, 3):
        landed(q_cols((y + 4 - d) % 4), rs7.at[d - 1])

    def collect(hh, carry):
        for t in range(2):
            i = hh * 2 + t
            out = (gk_out, gv_out)[t]
            for d in (1, 2, 3):
                landed(back_slot(out, hh, (y + 4 - d) % 4), rs9.at[i * 3 + d - 1])
            landed(back_slot(out, hh, y), ls9.at[i])
        return carry

    lax.fori_loop(0, 3, collect, 0)
    for e in range(2):
        landed(gw_cols(z, e), lsw.at[e])
        for d in (1, 2, 3):
            landed(gw_cols((z + 4 - d) % 4, e), rs13.at[(d - 1) * 2 + e])

    @pl.when(z == y)
    def _():
        for n in range(3):
            landed(w_hbm, ssw1.at[n])

    for n in range(3):
        landed(w_own, ssw2.at[n])

    def left_head(hh, carry):
        for t in range(3):
            for d in (1, 2, 3):
                landed(slot(t, hh, y), ss1.at[(hh * 3 + t) * 3 + d - 1])
        landed(q_half(hh, xh), ss2.at[hh])
        landed(oxs.at[hh], ss4.at[hh])
        landed(sxs.at[hh], ss4.at[hh + 3])
        for t in range(2):
            for d in (1, 2, 3):
                landed(fin.at[hh, 0:TOK, :], ss9.at[(hh * 2 + t) * 3 + d - 1])
        return carry

    lax.fori_loop(0, 3, left_head, 0)
    for n in range(6):
        landed(go_slot(y, 0), ss3.at[n])
    for n in range(4):
        landed(gxs.at[n], ss8.at[n])
        landed(cxs.at[n], ss8.at[n + 4])
        landed(dqxs.at[n], ss12.at[n])
        landed(cin.at[n], ss5.at[n])
    for n in range(3):
        landed(finq.at[n], ss7.at[n])
        landed(zin.at[n], ss11.at[n])
        landed(pin.at[0], ss10.at[n + 1])

    for n in range(1, 8):
        landed(pin.at[0], ss6.at[n])
    for n in range(6):
        landed(pin.at[0], ss13.at[n])


def local(query_rows, key_rows, value_rows, grad_out, w_out):
    any_spec = pl.BlockSpec(memory_space=pl.ANY)
    dma = pltpu.SemaphoreType.DMA
    vm = pltpu.VMEM
    rows = jax.ShapeDtypeStruct((1, TOK, HW), BF16)
    gq, gk, gv, gw = pl.pallas_call(
        kernel,
        out_shape=(rows, rows, rows, jax.ShapeDtypeStruct((96, D), BF16)),
        in_specs=[any_spec] * 5,
        out_specs=(any_spec,) * 4,
        scratch_shapes=[
            vm((3, 2 * HALF, HD), BF16),
            vm((3, HALF, HD), BF16),
            vm((3, HALF, HD), BF16),
            vm((3, HD, HALF), BF16),
            vm((3, HD, HALF), BF16),
            vm((HALF, D), BF16),
            vm((GW, D), BF16),
            vm((HALF, TOK), F32),
            vm((24, HALF, TOK), BF16),
            vm((GW, HALF), BF16),
            vm((3, 4, HD, TOK), F32),
            vm((3, 4, 8, TOK), F32),
            vm((3, 4, 8, TOK), F32),
            vm((3, 4, HD, TOK), BF16),
            vm((3, 4, HD, TOK), BF16),
            vm((3, 4, 8, TOK), F32),
            vm((3, 4, 8, TOK), F32),
            vm((4, 3, HD, TOK), BF16),
            vm((4, 3, 8, TOK), F32),
            vm((4, 3, HD, TOK), BF16),
            vm((4, 3, HD, TOK), BF16),
            vm((4, 3, 8, TOK), F32),
            vm((4, 3, 8, TOK), F32),
            vm((4, TOK, GW), F32),
            vm((4, TOK, GW), BF16),
            vm((4, TOK, GW), BF16),
            vm((4, TOK, GW), BF16),
            vm((3, HALF, HD), F32),
            vm((3, HALF, HD), F32),
            vm((6, HALF, HD), BF16),
            vm((4, 2, 2, 2, 96, GW), BF16),
            vm((4, 2, 2, 96, GW), BF16),
            vm((4, 2, 2, 96, GW), BF16),
            vm((3, 2, 2, 96, GW), BF16),
            vm((2, 2, 96, GW), BF16),
            vm((4, 96, GW), BF16),
            vm((4, 2, 96, GW), BF16),
            vm((8, GW, GW), F32),
            dma((27,)), dma((27,)), dma((9,)),
            dma((3,)), dma((3,)),
            dma((6,)), dma((6,)), dma((1,)),
            dma((3,)), dma((1,)), dma((3,)), dma((3,)),
            dma((6,)), dma((6,)),
            dma((4,)), dma((4,)),
            dma((8,)), dma((8,)),
            dma((3,)), dma((3,)), dma((1,)),
            dma((8,)), dma((8,)),
            dma((18,)), dma((18,)), dma((6,)),
            dma((4,)), dma((4,)),
            dma((3,)), dma((3,)),
            dma((4,)), dma((4,)),
            dma((6,)), dma((6,)), dma((2,)),
        ],
        compiler_params=pltpu.CompilerParams(
            has_side_effects=True, collective_id=0, vmem_limit_bytes=60 * 1024 * 1024
        ),
    )(query_rows, key_rows, value_rows, grad_out, w_out)
    return gq, gk, gv, gw.astype(F32)


def solution(mesh):
    in_specs = (
        P("fsdp", "rows", None),
        P("fsdp", "rows", None),
        P("fsdp", "rows", None),
        P("fsdp", "rows", None),
        P("fsdp", None),
    )
    out_specs = (
        P("fsdp", "rows", None),
        P("fsdp", "rows", None),
        P("fsdp", "rows", None),
        P("fsdp", None),
    )
    return jax.shard_map(local, mesh=mesh, in_specs=in_specs, out_specs=out_specs, check_vma=False)
```

```python
import math

import jax
import jax.numpy as jnp
from jax import lax
from jax.experimental import pallas as pl
from jax.experimental.pallas import tpu as pltpu
from jax.sharding import PartitionSpec as P

F32 = jnp.float32
BF16 = jnp.bfloat16
MESH = pl.DeviceIdType.MESH
D = 3072
HW = 1536
HD = 128
TOK = 256
GW = 384
HALF = 1024
KC = 256
NK = HALF // KC
SCALE = 1.0 / math.sqrt(HD)
CST = SCALE * math.log2(math.e)


def m128(x):
    return pl.multiple_of(x, 128)


def m256(x):
    return pl.multiple_of(x, 256)


def local_copy(src, dst, sem):
    return pltpu.make_async_copy(src, dst, sem)


def remote(src, dst, send_sem, recv_sem, dev):
    return pltpu.make_async_remote_copy(
        src_ref=src, dst_ref=dst, send_sem=send_sem, recv_sem=recv_sem,
        device_id=dev, device_id_type=MESH,
    )


def landed(ref, sem):
    pltpu.make_async_copy(ref, ref, sem).wait()


def dot(a, b):
    return jnp.dot(a, b, preferred_element_type=F32)


def kernel(
    q_hbm, k_hbm, v_hbm, go_hbm, w_hbm,
    gq_out, gk_out, gv_out, gw_out,
    qbuf, kbuf, vbuf, ktb, vtb, go, wbuf, sbuf, pbuf, att, obuf, stat, rbuf,
    oxs, oxr, sxs, sxr, g1, c1, gxs, gxr, cxs, cxr, dqk, dqxs, dqxr, finq,
    dkacc, dvacc, fin, termb, cin, zsum, zin, part, pin, redb, tacc,
    ss1, rs1, ls1, ss2, rs2, ss3, rs3, lsg, ssw1, rsw1, ssw2, rsw2,
    ss4, rs4, ss5, rs5, ss6, rs6, ss7, rs7, ls7, ss8, rs8, ss9, rs9, ls9,
    ss10, rs10, ss11, rs11, ss12, rs12,
):
    f = lax.axis_index("fsdp")
    r = lax.axis_index("rows")
    z, xl, c = f // 4, (f // 2) % 2, f % 2
    y, xh = r // 2, r % 2
    j = f % 4

    def dev(z_, xl_, c_, y_, xh_):
        return (z_ * 4 + xl_ * 2 + c_, y_ * 2 + xh_)

    def ydev(y_):
        return dev(z, xl, c, y_, xh)

    partner = dev(z, xl, c, y, 1 - xh)
    coremate = dev(z, xl, 1 - c, y, xh)
    ins = (k_hbm, v_hbm, q_hbm)

    def slot(t, hh, ys):
        if t == 2:
            return qbuf.at[hh, pl.ds(m256((xh * 4 + ys) * TOK), TOK), :]
        return (kbuf, vbuf)[t].at[hh, pl.ds(m256(ys * TOK), TOK), :]

    def cols(t, hh, yd):
        return ins[t].at[0, :, pl.ds(m128(yd * GW + hh * HD), HD)]

    def w_rows(n):
        return wbuf.at[pl.ds(pl.multiple_of(n * 96, 32), 96), :]

    w_own = w_rows(j)

    barrier = pltpu.get_barrier_semaphore()

    def hello(d):
        pl.semaphore_signal(barrier, inc=1, device_id=d, device_id_type=MESH)

    for d in (1, 2, 3):
        hello(ydev((y + d) % 4))
        hello(dev(z, xl, c, (y + d) % 4, 1 - xh))
        hello(dev((z + d) % 4, xl, c, y, xh))
        hello(dev(z, (xl + d // 2) % 2, c, y, (xh + d % 2) % 2))
    hello(coremate)
    pl.semaphore_wait(barrier, 13)

    @pl.when(z == y)
    def _():
        local_copy(w_hbm, w_own, rsw1.at[0]).start()
        for dz in (1, 2, 3):
            remote(w_hbm, w_own, ssw1.at[dz - 1], rsw1.at[0], dev((z + dz) % 4, xl, c, y, xh)).start()

    def send_head(hh, carry):
        for t in (2, 0, 1):
            for d in (1, 3, 2):
                yd = (y + d) % 4
                i = (hh * 3 + t) * 3 + d - 1
                remote(cols(t, hh, yd), slot(t, hh, y), ss1.at[i], rs1.at[i], ydev(yd)).start()
            local_copy(cols(t, hh, y), slot(t, hh, y), ls1.at[hh * 3 + t]).start()
        return carry

    lax.fori_loop(0, 3, send_head, 0)

    def go_slot(ys, h, n=1):
        return go.at[pl.ds(pl.multiple_of(ys * TOK + h * 128, 128), 128 * n), :]

    def go_src(h):
        return go_hbm.at[0, pl.ds(h * 128, 128), :]

    yr, yl = (y + 1) % 4, (y + 3) % 4
    yo = (y + 2) % 4
    remote(go_src(0), go_slot(y, 0), ss3.at[0], rs3.at[0], ydev(yr)).start()
    remote(go_src(1), go_slot(y, 1), ss3.at[2], rs3.at[2], ydev(yl)).start()
    remote(go_src(1), go_slot(y, 1), ss3.at[1], rs3.at[1], ydev(yr)).start()
    remote(go_src(0), go_slot(y, 0), ss3.at[3], rs3.at[3], ydev(yl)).start()
    local_copy(go_hbm.at[0], go_slot(y, 0, 2), lsg.at[0]).start()

    def arrived(t, hh):
        local_copy(cols(t, hh, y), slot(t, hh, y), ls1.at[hh * 3 + t]).wait()
        for d in (1, 3, 2):
            landed(slot(t, hh, (y + 4 - d) % 4), rs1.at[(hh * 3 + t) * 3 + d - 1])

    def q_half(hh, h):
        return qbuf.at[hh, pl.ds(pl.multiple_of(h * HALF, HALF), HALF), :]

    def relay(hh, carry):
        arrived(2, hh)
        remote(q_half(hh, xh), q_half(hh, xh), ss2.at[hh], rs2.at[hh], partner).start()
        return carry

    lax.fori_loop(0, 3, relay, 0)

    landed(w_own, rsw1.at[0])
    remote(w_own, w_own, ssw2.at[0], rsw2.at[0], coremate).start()
    remote(w_own, w_own, ssw2.at[1], rsw2.at[1], dev(z, 1 - xl, c, y, xh)).start()

    def scores_block(hh, s):
        i = hh * 8 + s
        qt = qbuf[hh, pl.ds(m256(s * TOK), TOK), :].T
        m = jnp.full((1, TOK), -jnp.inf, F32)
        for kc in range(NK):
            ks = slice(kc * KC, (kc + 1) * KC)
            sc = dot(kbuf[hh, ks, :], qt)
            sbuf[ks, :] = sc
            m = jnp.maximum(m, jnp.max(sc, axis=0, keepdims=True))
        mc = m * CST
        l = jnp.zeros((1, TOK), F32)
        o = jnp.zeros((HD, TOK), F32)
        for kc in range(NK):
            ks = slice(kc * KC, (kc + 1) * KC)
            p = jnp.exp2(sbuf[ks, :] * CST - mc)
            l = l + jnp.sum(p, axis=0, keepdims=True)
            pb = p.astype(BF16)
            pbuf[i, ks, :] = pb
            o = o + dot(vtb[hh, :, ks], pb)
        return m, l, o

    def forward(hh, carry):
        arrived(0, hh)
        arrived(1, hh)
        for kc in range(NK):
            ks = slice(kc * KC, (kc + 1) * KC)
            ktb[hh, :, ks] = kbuf[hh, ks, :].T
            vtb[hh, :, ks] = vbuf[hh, ks, :].T
        landed(q_half(hh, 1 - xh), rs2.at[hh])

        def theirs(ys, carry):
            m, l, o = scores_block(hh, (1 - xh) * 4 + ys)
            oxs[hh, ys] = o.astype(BF16)
            sxs[hh, ys, 0:1, :] = m
            sxs[hh, ys, 1:2, :] = l
            return carry

        lax.fori_loop(0, 4, theirs, 0)
        remote(oxs.at[hh], oxr.at[hh], ss4.at[hh], rs4.at[hh], partner).start()
        remote(sxs.at[hh], sxr.at[hh], ss4.at[hh + 3], rs4.at[hh + 3], partner).start()

        def mine(ys, carry):
            m, l, o = scores_block(hh, xh * 4 + ys)
            obuf[hh, ys] = o
            stat[hh, ys, 0:1, :] = m
            stat[hh, ys, 1:2, :] = l
            return carry

        return lax.fori_loop(0, 4, mine, carry)

    lax.fori_loop(0, 3, forward, 0)

    w_across = w_rows((1 - xl) * 2 + c)
    landed(w_across, rsw2.at[1])
    remote(w_across, w_across, ssw2.at[2], rsw2.at[2], coremate).start()

    def merge(hh, carry):
        landed(oxr.at[hh], rs4.at[hh])
        landed(sxr.at[hh], rs4.at[hh + 3])

        def block(ys, carry):
            ma, la = stat[hh, ys, 0:1, :], stat[hh, ys, 1:2, :]
            mb, lb = sxr[hh, ys, 0:1, :], sxr[hh, ys, 1:2, :]
            m = jnp.maximum(ma, mb)
            ea, eb = jnp.exp2((ma - m) * CST), jnp.exp2((mb - m) * CST)
            inv = 1.0 / (la * ea + lb * eb)
            ra, rb = ea * inv, eb * inv
            o = obuf[hh, ys] * ra + oxr[hh, ys].astype(F32) * rb
            obuf[hh, ys] = o
            att[pl.ds(m128(hh * HD), HD), pl.ds(m256(ys * TOK), TOK)] = o.astype(BF16)
            rbuf[hh, ys, 0:1, :] = ra
            rbuf[hh, ys, 1:2, :] = rb
            return carry

        return lax.fori_loop(0, 4, block, carry)

    lax.fori_loop(0, 3, merge, 0)
    landed(w_rows(xl * 2 + 1 - c), rsw2.at[0])
    landed(w_rows((1 - xl) * 2 + 1 - c), rsw2.at[2])

    def project(ys):
        g = lax.dot_general(
            wbuf[...], go[pl.ds(m256(ys * TOK), TOK), :], (((1,), (1,)), ((), ())), preferred_element_type=F32
        )
        for hh in range(3):
            gh = g[hh * HD : (hh + 1) * HD, :]
            cen = jnp.sum(gh * obuf[hh, ys], axis=0, keepdims=True)
            ra, rb = rbuf[hh, ys, 0:1, :], rbuf[hh, ys, 1:2, :]
            g1[ys, hh] = (gh * ra).astype(BF16)
            gxs[ys, hh] = (gh * rb).astype(BF16)
            c1[ys, hh, 0:1, :] = cen * ra
            cxs[ys, hh, 0:1, :] = cen * rb
        remote(gxs.at[ys], gxr.at[ys], ss8.at[ys], rs8.at[ys], partner).start()
        remote(cxs.at[ys], cxr.at[ys], ss8.at[ys + 4], rs8.at[ys + 4], partner).start()

    dkacc[...] = jnp.zeros_like(dkacc)
    dvacc[...] = jnp.zeros_like(dvacc)

    def backward(own, ys, after=None):
        s = (xh if own else 1 - xh) * 4 + ys

        def head(hh, carry):
            i = hh * 8 + s
            qn = qbuf[hh, pl.ds(m256(s * TOK), TOK), :]
            gt = (g1 if own else gxr)[ys, hh]
            cen = (c1 if own else cxr)[ys, hh, 0:1, :]
            gn = gt.T
            dq = jnp.zeros((HD, TOK), F32)
            for kc in range(NK):
                ks = slice(kc * KC, (kc + 1) * KC)
                dp = dot(vbuf[hh, ks, :], gt)
                pb = pbuf[i, ks, :]
                ds = (pb.astype(F32) * (dp - cen)).astype(BF16)
                dq = dq + dot(ktb[hh, :, ks], ds)
                dkacc[hh, ks, :] += dot(ds, qn)
                dvacc[hh, ks, :] += dot(pb, gn)
            dqn = (dq * SCALE).T
            hs = pl.ds(m128(hh * HD), HD)
            if own:
                dqk[ys, :, hs] = dqn
            else:
                dqxs[ys, :, hs] = dqn.astype(BF16)
            if after is not None:
                after(hh)
            return carry

        lax.fori_loop(0, 3, head, 0)

    def theirs_in(ys):
        landed(gxr.at[ys], rs8.at[ys])
        landed(cxr.at[ys], rs8.at[ys + 4])

    def send_dq(ys):
        remote(dqxs.at[ys], dqxr.at[ys], ss12.at[ys], rs12.at[ys], partner).start()

    def q_cols(ysrc):
        return gq_out.at[0, :, pl.ds(m128(ysrc * GW), GW)]

    def finish_q(d):
        ys = (y + d) % 4
        landed(dqxr.at[ys], rs12.at[ys])
        finq[ys] = (dqk[ys] + dqxr[ys].astype(F32)).astype(BF16)
        if d == 0:
            local_copy(finq.at[ys], q_cols(y), ls7.at[0]).start()
        else:
            remote(finq.at[ys], q_cols(y), ss7.at[d - 1], rs7.at[d - 1], ydev(ys)).start()

    local_copy(go_hbm.at[0], go_slot(y, 0, 2), lsg.at[0]).wait()
    project(y)
    backward(True, y)

    landed(go_slot(yl, 0), rs3.at[0])
    remote(go_slot(yl, 0), go_slot(yl, 0), ss3.at[4], rs3.at[4], ydev(yr)).start()
    landed(go_slot(yr, 1), rs3.at[2])
    remote(go_slot(yr, 1), go_slot(yr, 1), ss3.at[5], rs3.at[5], ydev(yl)).start()

    theirs_in(y)
    backward(False, y)
    send_dq(y)

    def term_cols(zd, xd):
        return pl.ds(m128((zd * 2 + xd) * GW), GW)

    def term_dot(ys, zd, xd):
        at = pl.ds(m256(ys * TOK), TOK)
        return dot(att[:, at], go[at, term_cols(zd, xd)])

    def term_part(ys, first=False):
        def add(n, carry):
            t = term_dot(ys, n // 2, n % 2)
            tacc[n] = t if first else tacc[n] + t
            return carry

        lax.fori_loop(0, 8, add, 0)

    term_part(y, True)
    landed(go_slot(yl, 1), rs3.at[1])
    project(yl)
    backward(True, yl)
    landed(go_slot(yr, 0), rs3.at[3])
    project(yr)
    theirs_in(yl)
    backward(False, yl)
    send_dq(yl)
    backward(True, yr)
    theirs_in(yr)
    backward(False, yr)
    send_dq(yr)
    term_part(yl)
    term_part(yr)
    finish_q(0)

    landed(go_slot(yo, 0), rs3.at[4])
    landed(go_slot(yo, 1), rs3.at[5])
    project(yo)

    def term(o, carry):
        zd = (z + 1 + o) % 4
        for xd in range(2):
            t = (tacc[zd * 2 + xd] + term_dot(yo, zd, xd)).astype(BF16)
            for n in range(4):
                termb[zd, n % 2, xd, n // 2] = t[n * 96 : (n + 1) * 96, :]
        remote(termb.at[zd, 1 - c], cin.at[zd], ss5.at[zd], rs5.at[zd], coremate).start()
        return carry

    lax.fori_loop(0, 4, term, 0)
    finish_q(3)
    finish_q(1)
    backward(True, yo)

    def back_slot(out, hh, ysrc):
        return out.at[0, :, pl.ds(m128(ysrc * GW + hh * HD), HD)]

    def hand_out(hh):
        for t in range(2):
            i = hh * 2 + t
            fin[i] = ((dkacc, dvacc)[t][hh] * (SCALE, 1.0)[t]).astype(BF16)
            out = (gk_out, gv_out)[t]
            for d in (1, 3, 2):
                yd = (y + d) % 4
                n = i * 3 + d - 1
                remote(fin.at[i, pl.ds(m256(yd * TOK), TOK), :], back_slot(out, hh, y), ss9.at[n], rs9.at[n],
                       ydev(yd)).start()
            local_copy(fin.at[i, pl.ds(m256(y * TOK), TOK), :], back_slot(out, hh, y), ls9.at[i]).start()

    theirs_in(yo)
    backward(False, yo, hand_out)
    send_dq(yo)

    def to_z(o, carry):
        zd = (z + 1 + o) % 4
        landed(cin.at[zd], rs5.at[zd])
        for e in range(2):
            for a in range(2):
                t = termb[zd, c, e, a].astype(F32) + cin[zd, e, a].astype(F32)
                zsum[o, e, a] = t.astype(BF16)

        @pl.when(o < 3)
        def _():
            remote(zsum.at[o], zin.at[o], ss11.at[o], rs11.at[o], dev(zd, xl, c, y, xh)).start()

        return carry

    lax.fori_loop(0, 4, to_z, 0)

    for i in range(3):
        landed(zin.at[i], rs11.at[i])
    for e in range(2):
        for a in range(2):
            t = zsum[3, e, a].astype(F32)
            for i in range(3):
                t = t + zin[i, e, a].astype(F32)
            part[e, a] = t.astype(BF16)
    for n in (1, 2, 3):
        a, e = n // 2, n % 2
        xld, xhd = (xl + a) % 2, (xh + e) % 2
        remote(part.at[xhd, xld], pin.at[n], ss10.at[n], rs10.at[n], dev(z, xld, c, y, xhd)).start()
    finish_q(2)

    acc = part[xh, xl].astype(F32)
    for n in (1, 2, 3):
        landed(pin.at[n], rs10.at[n])
        acc = acc + pin[n].astype(F32)
    redb[...] = acc.astype(BF16)

    def gw_cols(zs, e):
        return gw_out.at[:, pl.ds(m128((zs * 2 + e) * GW), GW)]

    own = z * 2 + xh
    for n in range(8):
        d, e = n // 2, n % 2
        yd, xd = (y + d) % 4, (xh + e) % 2

        def to_owner():
            remote(redb, gw_cols(z, xh), ss6.at[n], rs6.at[own], dev(y, xl, c, yd, xd)).start()

        if n == 0:
            pl.when(z != y)(to_owner)

            @pl.when(z == y)
            def _():
                local_copy(redb, gw_cols(z, xh), rs6.at[own]).start()
        else:
            to_owner()

    landed(q_cols(y), ls7.at[0])
    for d in (1, 2, 3):
        landed(q_cols((y + 4 - d) % 4), rs7.at[d - 1])

    def collect(hh, carry):
        for t in range(2):
            i = hh * 2 + t
            out = (gk_out, gv_out)[t]
            for d in (1, 2, 3):
                landed(back_slot(out, hh, (y + 4 - d) % 4), rs9.at[i * 3 + d - 1])
            landed(back_slot(out, hh, y), ls9.at[i])
        return carry

    lax.fori_loop(0, 3, collect, 0)
    for n in range(8):
        landed(gw_cols(n // 2, n % 2), rs6.at[n])

    @pl.when(z == y)
    def _():
        for n in range(3):
            landed(w_hbm, ssw1.at[n])

    for n in range(3):
        landed(w_own, ssw2.at[n])

    def left_head(hh, carry):
        for t in range(3):
            for d in (1, 2, 3):
                landed(slot(t, hh, y), ss1.at[(hh * 3 + t) * 3 + d - 1])
        landed(q_half(hh, xh), ss2.at[hh])
        landed(oxs.at[hh], ss4.at[hh])
        landed(sxs.at[hh], ss4.at[hh + 3])
        for t in range(2):
            for d in (1, 2, 3):
                landed(fin.at[hh, 0:TOK, :], ss9.at[(hh * 2 + t) * 3 + d - 1])
        return carry

    lax.fori_loop(0, 3, left_head, 0)
    for n in range(6):
        landed(go_slot(y, 0), ss3.at[n])
    for n in range(4):
        landed(gxs.at[n], ss8.at[n])
        landed(cxs.at[n], ss8.at[n + 4])
        landed(dqxs.at[n], ss12.at[n])
        landed(cin.at[n], ss5.at[n])
    for n in range(3):
        landed(finq.at[n], ss7.at[n])
        landed(zin.at[n], ss11.at[n])
        landed(pin.at[0], ss10.at[n + 1])

    @pl.when(z != y)
    def _():
        landed(redb, ss6.at[0])

    for n in range(1, 8):
        landed(redb, ss6.at[n])


def store(gq, gk, gv, gw, gq_out, gk_out, gv_out, gw_out):
    gq_out[...] = gq[...]
    gk_out[...] = gk[...]
    gv_out[...] = gv[...]
    gw_out[...] = gw[...].astype(F32)


def local(query_rows, key_rows, value_rows, grad_out, w_out):
    any_spec = pl.BlockSpec(memory_space=pl.ANY)
    dma = pltpu.SemaphoreType.DMA
    vm = pltpu.VMEM
    rows = jax.ShapeDtypeStruct((1, TOK, HW), BF16)
    gq, gk, gv, gw = pl.pallas_call(
        kernel,
        out_shape=(rows, rows, rows, jax.ShapeDtypeStruct((96, D), BF16)),
        in_specs=[any_spec] * 5,
        out_specs=(any_spec,) * 4,
        scratch_shapes=[
            vm((3, 2 * HALF, HD), BF16),
            vm((3, HALF, HD), BF16),
            vm((3, HALF, HD), BF16),
            vm((3, HD, HALF), BF16),
            vm((3, HD, HALF), BF16),
            vm((HALF, D), BF16),
            vm((GW, D), BF16),
            vm((HALF, TOK), F32),
            vm((24, HALF, TOK), BF16),
            vm((GW, HALF), BF16),
            vm((3, 4, HD, TOK), F32),
            vm((3, 4, 8, TOK), F32),
            vm((3, 4, 8, TOK), F32),
            vm((3, 4, HD, TOK), BF16),
            vm((3, 4, HD, TOK), BF16),
            vm((3, 4, 8, TOK), F32),
            vm((3, 4, 8, TOK), F32),
            vm((4, 3, HD, TOK), BF16),
            vm((4, 3, 8, TOK), F32),
            vm((4, 3, HD, TOK), BF16),
            vm((4, 3, HD, TOK), BF16),
            vm((4, 3, 8, TOK), F32),
            vm((4, 3, 8, TOK), F32),
            vm((4, TOK, GW), F32),
            vm((4, TOK, GW), BF16),
            vm((4, TOK, GW), BF16),
            vm((4, TOK, GW), BF16),
            vm((3, HALF, HD), F32),
            vm((3, HALF, HD), F32),
            vm((6, HALF, HD), BF16),
            vm((4, 2, 2, 2, 96, GW), BF16),
            vm((4, 2, 2, 96, GW), BF16),
            vm((4, 2, 2, 96, GW), BF16),
            vm((3, 2, 2, 96, GW), BF16),
            vm((2, 2, 96, GW), BF16),
            vm((4, 96, GW), BF16),
            vm((96, GW), BF16),
            vm((8, GW, GW), F32),
            dma((27,)), dma((27,)), dma((9,)),
            dma((3,)), dma((3,)),
            dma((6,)), dma((6,)), dma((1,)),
            dma((3,)), dma((1,)), dma((3,)), dma((3,)),
            dma((6,)), dma((6,)),
            dma((4,)), dma((4,)),
            dma((8,)), dma((8,)),
            dma((3,)), dma((3,)), dma((1,)),
            dma((8,)), dma((8,)),
            dma((18,)), dma((18,)), dma((6,)),
            dma((4,)), dma((4,)),
            dma((3,)), dma((3,)),
            dma((4,)), dma((4,)),
        ],
        compiler_params=pltpu.CompilerParams(
            has_side_effects=True, collective_id=0, vmem_limit_bytes=60 * 1024 * 1024
        ),
    )(query_rows, key_rows, value_rows, grad_out, w_out)
    half = pl.BlockSpec((1, TOK // 2, HW), lambda i: (0, i, 0))
    part = pl.BlockSpec((48, D), lambda i: (i, 0))
    return pl.pallas_call(
        store,
        out_shape=(rows, rows, rows, jax.ShapeDtypeStruct((96, D), F32)),
        grid=(2,),
        in_specs=[half] * 3 + [part],
        out_specs=[half] * 3 + [part],
    )(gq, gk, gv, gw)


def solution(mesh):
    in_specs = (
        P("fsdp", "rows", None),
        P("fsdp", "rows", None),
        P("fsdp", "rows", None),
        P("fsdp", "rows", None),
        P("fsdp", None),
    )
    out_specs = (
        P("fsdp", "rows", None),
        P("fsdp", "rows", None),
        P("fsdp", "rows", None),
        P("fsdp", None),
    )
    return jax.shard_map(local, mesh=mesh, in_specs=in_specs, out_specs=out_specs, check_vma=False)
```

```python
import math

import jax
import jax.numpy as jnp
from jax import lax
from jax.experimental import pallas as pl
from jax.experimental.pallas import tpu as pltpu
from jax.sharding import PartitionSpec as P

F32 = jnp.float32
BF16 = jnp.bfloat16
MESH = pl.DeviceIdType.MESH
D = 3072
HW = 1536
HD = 128
TOK = 256
GW = 384
HALF = 1024
KC = 256
NK = HALF // KC
SCALE = 1.0 / math.sqrt(HD)
CST = SCALE * math.log2(math.e)


def m128(x):
    return pl.multiple_of(x, 128)


def m256(x):
    return pl.multiple_of(x, 256)


def local_copy(src, dst, sem):
    return pltpu.make_async_copy(src, dst, sem)


def remote(src, dst, send_sem, recv_sem, dev):
    return pltpu.make_async_remote_copy(
        src_ref=src, dst_ref=dst, send_sem=send_sem, recv_sem=recv_sem,
        device_id=dev, device_id_type=MESH,
    )


def landed(ref, sem):
    pltpu.make_async_copy(ref, ref, sem).wait()


def dot(a, b):
    return jnp.dot(a, b, preferred_element_type=F32)


def kernel(
    q_hbm, k_hbm, v_hbm, go_hbm, w_hbm,
    gq_out, gk_out, gv_out, gw_out,
    qbuf, kbuf, vbuf, ktb, vtb, go, wbuf, sbuf, pbuf, att, obuf, stat, rbuf,
    oxs, oxr, sxs, sxr, g1, c1, gxs, gxr, cxs, cxr, dqk, dqxs, dqxr, finq,
    dkacc, dvacc, fin, termb, cin, zsum, zin, xsum, xin, hsum, hin, part, pin, redb, tacc,
    ss1, rs1, ls1, ss2, rs2, ss3, rs3, lsg, ssw1, rsw1, ssw2, rsw2,
    ss4, rs4, ss5, rs5, ss6, rs6, ss7, rs7, ls7, ss8, rs8, ss9, rs9, ls9,
    ss10, rs10, ss11, rs11, ss12, rs12, ss13, rs13, ss14, rs14,
):
    f = lax.axis_index("fsdp")
    r = lax.axis_index("rows")
    z, xl, c = f // 4, (f // 2) % 2, f % 2
    y, xh = r // 2, r % 2
    j = f % 4

    def dev(z_, xl_, c_, y_, xh_):
        return (z_ * 4 + xl_ * 2 + c_, y_ * 2 + xh_)

    def ydev(y_):
        return dev(z, xl, c, y_, xh)

    partner = dev(z, xl, c, y, 1 - xh)
    coremate = dev(z, xl, 1 - c, y, xh)
    ins = (k_hbm, v_hbm, q_hbm)

    def slot(t, hh, ys):
        if t == 2:
            return qbuf.at[hh, pl.ds(m256((xh * 4 + ys) * TOK), TOK), :]
        return (kbuf, vbuf)[t].at[hh, pl.ds(m256(ys * TOK), TOK), :]

    def cols(t, hh, yd):
        return ins[t].at[0, :, pl.ds(m128(yd * GW + hh * HD), HD)]

    def w_rows(n):
        return wbuf.at[pl.ds(pl.multiple_of(n * 96, 32), 96), :]

    w_own = w_rows(j)

    barrier = pltpu.get_barrier_semaphore()

    def hello(d):
        pl.semaphore_signal(barrier, inc=1, device_id=d, device_id_type=MESH)

    for d in (1, 2, 3):
        hello(ydev((y + d) % 4))
        hello(dev(z, xl, c, (y + d) % 4, 1 - xh))
        hello(dev((z + d) % 4, xl, c, y, xh))
        hello(dev(z, (xl + d // 2) % 2, c, y, (xh + d % 2) % 2))
    hello(coremate)
    pl.semaphore_wait(barrier, 13)

    @pl.when(z == y)
    def _():
        local_copy(w_hbm, w_own, rsw1.at[0]).start()
        for dz in (1, 2, 3):
            remote(w_hbm, w_own, ssw1.at[dz - 1], rsw1.at[0], dev((z + dz) % 4, xl, c, y, xh)).start()

    def send_head(hh, carry):
        for t in (2, 0, 1):
            for d in (1, 3, 2):
                yd = (y + d) % 4
                i = (hh * 3 + t) * 3 + d - 1
                remote(cols(t, hh, yd), slot(t, hh, y), ss1.at[i], rs1.at[i], ydev(yd)).start()
            local_copy(cols(t, hh, y), slot(t, hh, y), ls1.at[hh * 3 + t]).start()
        return carry

    lax.fori_loop(0, 3, send_head, 0)

    def go_slot(ys, h, n=1):
        return go.at[pl.ds(pl.multiple_of(ys * TOK + h * 128, 128), 128 * n), :]

    def go_src(h):
        return go_hbm.at[0, pl.ds(h * 128, 128), :]

    yr, yl = (y + 1) % 4, (y + 3) % 4
    yo = (y + 2) % 4
    remote(go_src(0), go_slot(y, 0), ss3.at[0], rs3.at[0], ydev(yr)).start()
    remote(go_src(1), go_slot(y, 1), ss3.at[2], rs3.at[2], ydev(yl)).start()
    remote(go_src(1), go_slot(y, 1), ss3.at[1], rs3.at[1], ydev(yr)).start()
    remote(go_src(0), go_slot(y, 0), ss3.at[3], rs3.at[3], ydev(yl)).start()
    local_copy(go_hbm.at[0], go_slot(y, 0, 2), lsg.at[0]).start()

    def arrived(t, hh):
        local_copy(cols(t, hh, y), slot(t, hh, y), ls1.at[hh * 3 + t]).wait()
        for d in (1, 3, 2):
            landed(slot(t, hh, (y + 4 - d) % 4), rs1.at[(hh * 3 + t) * 3 + d - 1])

    def q_half(hh, h):
        return qbuf.at[hh, pl.ds(pl.multiple_of(h * HALF, HALF), HALF), :]

    def relay(hh, carry):
        arrived(2, hh)
        remote(q_half(hh, xh), q_half(hh, xh), ss2.at[hh], rs2.at[hh], partner).start()
        return carry

    lax.fori_loop(0, 3, relay, 0)

    landed(w_own, rsw1.at[0])
    remote(w_own, w_own, ssw2.at[0], rsw2.at[0], coremate).start()
    remote(w_own, w_own, ssw2.at[1], rsw2.at[1], dev(z, 1 - xl, c, y, xh)).start()

    def scores_block(hh, s):
        i = hh * 8 + s
        qt = qbuf[hh, pl.ds(m256(s * TOK), TOK), :].T
        m = jnp.full((1, TOK), -jnp.inf, F32)
        for kc in range(NK):
            ks = slice(kc * KC, (kc + 1) * KC)
            sc = dot(kbuf[hh, ks, :], qt)
            sbuf[ks, :] = sc
            m = jnp.maximum(m, jnp.max(sc, axis=0, keepdims=True))
        mc = m * CST
        l = jnp.zeros((1, TOK), F32)
        o = jnp.zeros((HD, TOK), F32)
        for kc in range(NK):
            ks = slice(kc * KC, (kc + 1) * KC)
            p = jnp.exp2(sbuf[ks, :] * CST - mc)
            l = l + jnp.sum(p, axis=0, keepdims=True)
            pb = p.astype(BF16)
            pbuf[i, ks, :] = pb
            o = o + dot(vtb[hh, :, ks], pb)
        return m, l, o

    def forward(hh, carry):
        arrived(0, hh)
        arrived(1, hh)
        for kc in range(NK):
            ks = slice(kc * KC, (kc + 1) * KC)
            ktb[hh, :, ks] = kbuf[hh, ks, :].T
            vtb[hh, :, ks] = vbuf[hh, ks, :].T
        landed(q_half(hh, 1 - xh), rs2.at[hh])

        def theirs(ys, carry):
            m, l, o = scores_block(hh, (1 - xh) * 4 + ys)
            oxs[hh, ys] = o.astype(BF16)
            sxs[hh, ys, 0:1, :] = m
            sxs[hh, ys, 1:2, :] = l
            return carry

        lax.fori_loop(0, 4, theirs, 0)
        remote(oxs.at[hh], oxr.at[hh], ss4.at[hh], rs4.at[hh], partner).start()
        remote(sxs.at[hh], sxr.at[hh], ss4.at[hh + 3], rs4.at[hh + 3], partner).start()

        def mine(ys, carry):
            m, l, o = scores_block(hh, xh * 4 + ys)
            obuf[hh, ys] = o
            stat[hh, ys, 0:1, :] = m
            stat[hh, ys, 1:2, :] = l
            return carry

        return lax.fori_loop(0, 4, mine, carry)

    lax.fori_loop(0, 3, forward, 0)

    w_across = w_rows((1 - xl) * 2 + c)
    landed(w_across, rsw2.at[1])
    remote(w_across, w_across, ssw2.at[2], rsw2.at[2], coremate).start()

    def merge(hh, carry):
        landed(oxr.at[hh], rs4.at[hh])
        landed(sxr.at[hh], rs4.at[hh + 3])

        def block(ys, carry):
            ma, la = stat[hh, ys, 0:1, :], stat[hh, ys, 1:2, :]
            mb, lb = sxr[hh, ys, 0:1, :], sxr[hh, ys, 1:2, :]
            m = jnp.maximum(ma, mb)
            ea, eb = jnp.exp2((ma - m) * CST), jnp.exp2((mb - m) * CST)
            inv = 1.0 / (la * ea + lb * eb)
            ra, rb = ea * inv, eb * inv
            o = obuf[hh, ys] * ra + oxr[hh, ys].astype(F32) * rb
            obuf[hh, ys] = o
            att[pl.ds(m128(hh * HD), HD), pl.ds(m256(ys * TOK), TOK)] = o.astype(BF16)
            rbuf[hh, ys, 0:1, :] = ra
            rbuf[hh, ys, 1:2, :] = rb
            return carry

        return lax.fori_loop(0, 4, block, carry)

    lax.fori_loop(0, 3, merge, 0)
    landed(w_rows(xl * 2 + 1 - c), rsw2.at[0])
    landed(w_rows((1 - xl) * 2 + 1 - c), rsw2.at[2])

    def project(ys):
        g = lax.dot_general(
            wbuf[...], go[pl.ds(m256(ys * TOK), TOK), :], (((1,), (1,)), ((), ())), preferred_element_type=F32
        )
        for hh in range(3):
            gh = g[hh * HD : (hh + 1) * HD, :]
            cen = jnp.sum(gh * obuf[hh, ys], axis=0, keepdims=True)
            ra, rb = rbuf[hh, ys, 0:1, :], rbuf[hh, ys, 1:2, :]
            g1[ys, hh] = (gh * ra).astype(BF16)
            gxs[ys, hh] = (gh * rb).astype(BF16)
            c1[ys, hh, 0:1, :] = cen * ra
            cxs[ys, hh, 0:1, :] = cen * rb
            i = ys * 3 + hh
            remote(gxs.at[ys, hh], gxr.at[ys, hh], ss8.at[i], rs8.at[i], partner).start()
            remote(cxs.at[ys, hh], cxr.at[ys, hh], ss8.at[i + 12], rs8.at[i + 12], partner).start()

    dkacc[...] = jnp.zeros_like(dkacc)
    dvacc[...] = jnp.zeros_like(dvacc)

    def one_head(own, ys, hh):
        s = (xh if own else 1 - xh) * 4 + ys
        i = hh * 8 + s
        qn = qbuf[hh, pl.ds(m256(s * TOK), TOK), :]
        gt = (g1 if own else gxr)[ys, hh]
        cen = (c1 if own else cxr)[ys, hh, 0:1, :]
        gn = gt.T
        dq = jnp.zeros((HD, TOK), F32)
        for kc in range(NK):
            ks = slice(kc * KC, (kc + 1) * KC)
            dp = dot(vbuf[hh, ks, :], gt)
            pb = pbuf[i, ks, :]
            ds = (pb.astype(F32) * (dp - cen)).astype(BF16)
            dq = dq + dot(ktb[hh, :, ks], ds)
            dkacc[hh, ks, :] += dot(ds, qn)
            dvacc[hh, ks, :] += dot(pb, gn)
        dqn = (dq * SCALE).T
        hs = pl.ds(m128(hh * HD), HD)
        if own:
            dqk[ys, :, hs] = dqn
        else:
            dqxs[ys, :, hs] = dqn.astype(BF16)

    def head_in(ys, hh):
        i = ys * 3 + hh
        landed(gxr.at[ys, hh], rs8.at[i])
        landed(cxr.at[ys, hh], rs8.at[i + 12])

    def backward(own, ys):
        def head(hh, carry):
            one_head(own, ys, hh)
            return carry

        lax.fori_loop(0, 3, head, 0)

    def theirs_in(ys):
        for hh in range(3):
            head_in(ys, hh)

    def send_dq(ys):
        remote(dqxs.at[ys], dqxr.at[ys], ss12.at[ys], rs12.at[ys], partner).start()

    def q_cols(ysrc):
        return gq_out.at[0, :, pl.ds(m128(ysrc * GW), GW)]

    def finish_q(d):
        ys = (y + d) % 4
        landed(dqxr.at[ys], rs12.at[ys])
        finq[ys] = (dqk[ys] + dqxr[ys].astype(F32)).astype(BF16)
        if d == 0:
            local_copy(finq.at[ys], q_cols(y), ls7.at[0]).start()
        else:
            remote(finq.at[ys], q_cols(y), ss7.at[d - 1], rs7.at[d - 1], ydev(ys)).start()

    local_copy(go_hbm.at[0], go_slot(y, 0, 2), lsg.at[0]).wait()
    project(y)
    backward(True, y)

    landed(go_slot(yl, 0), rs3.at[0])
    remote(go_slot(yl, 0), go_slot(yl, 0), ss3.at[4], rs3.at[4], ydev(yr)).start()
    landed(go_slot(yr, 1), rs3.at[2])
    remote(go_slot(yr, 1), go_slot(yr, 1), ss3.at[5], rs3.at[5], ydev(yl)).start()

    theirs_in(y)
    backward(False, y)
    send_dq(y)

    def term_cols(zd, xd):
        return pl.ds(m128((zd * 2 + xd) * GW), GW)

    def term_dot(ys, zd, xd):
        at = pl.ds(m256(ys * TOK), TOK)
        return dot(att[:, at], go[at, term_cols(zd, xd)])

    def term_part(ys, first=False):
        def add(n, carry):
            t = term_dot(ys, n // 2, n % 2)
            tacc[n] = t if first else tacc[n] + t
            return carry

        lax.fori_loop(0, 8, add, 0)

    term_part(y, True)
    landed(go_slot(yl, 1), rs3.at[1])
    project(yl)
    backward(True, yl)
    landed(go_slot(yr, 0), rs3.at[3])
    project(yr)
    theirs_in(yl)
    backward(False, yl)
    send_dq(yl)
    backward(True, yr)
    theirs_in(yr)
    backward(False, yr)
    send_dq(yr)
    term_part(yl)
    term_part(yr)
    finish_q(0)
    finish_q(3)
    finish_q(1)

    landed(go_slot(yo, 0), rs3.at[4])
    landed(go_slot(yo, 1), rs3.at[5])
    project(yo)

    def term(o, carry):
        zd = (z + 1 + o) % 4
        for xd in range(2):
            t = (tacc[zd * 2 + xd] + term_dot(yo, zd, xd)).astype(BF16)
            for n in range(4):
                termb[zd, n % 2, xd, n // 2] = t[n * 96 : (n + 1) * 96, :]
        remote(termb.at[zd, 1 - c], cin.at[zd], ss5.at[zd], rs5.at[zd], coremate).start()
        return carry

    lax.fori_loop(0, 4, term, 0)

    def back_slot(out, hh, ysrc):
        return out.at[0, :, pl.ds(m128(ysrc * GW + hh * HD), HD)]

    def hand_out(hh):
        for t in range(2):
            i = hh * 2 + t
            fin[i] = ((dkacc, dvacc)[t][hh] * (SCALE, 1.0)[t]).astype(BF16)
            out = (gk_out, gv_out)[t]
            for d in (1, 3, 2):
                yd = (y + d) % 4
                n = i * 3 + d - 1
                remote(fin.at[i, pl.ds(m256(yd * TOK), TOK), :], back_slot(out, hh, y), ss9.at[n], rs9.at[n],
                       ydev(yd)).start()
            local_copy(fin.at[i, pl.ds(m256(y * TOK), TOK), :], back_slot(out, hh, y), ls9.at[i]).start()

    backward(True, yo)

    def to_mates(o, carry):
        zd = (z + 1 + o) % 4
        landed(cin.at[zd], rs5.at[zd])
        for e in range(2):
            for a in range(2):
                t = (termb[zd, c, e, a].astype(F32) + cin[zd, e, a].astype(F32)).astype(BF16)
                zsum[o, e, a] = t[:48, :]
                xsum[e, a, zd] = t[48:, :]

        @pl.when(o < 3)
        def _():
            remote(zsum.at[o], zin.at[o], ss11.at[o], rs11.at[o], dev(zd, xl, c, y, xh)).start()

        return carry

    lax.fori_loop(0, 4, to_mates, 0)
    x_mates = [(n, (xl + n // 2) % 2, (xh + n % 2) % 2) for n in (1, 2, 3)]
    for n, xld, xhd in x_mates:
        remote(xsum.at[xhd, xld], xin.at[n], ss13.at[n], rs13.at[n], dev(z, xld, c, y, xhd)).start()

    def last_head(hh, carry):
        head_in(yo, hh)
        one_head(False, yo, hh)
        hand_out(hh)
        return carry

    lax.fori_loop(0, 3, last_head, 0)
    send_dq(yo)

    for n in (1, 2, 3):
        landed(xin.at[n], rs13.at[n])
    for zd in range(4):
        t = xsum[xh, xl, zd].astype(F32)
        for n in (1, 2, 3):
            t = t + xin[n, zd].astype(F32)
        hsum[zd] = t.astype(BF16)
    for d in (1, 2, 3):
        zd = (z + d) % 4
        remote(hsum.at[zd], hin.at[d], ss14.at[d], rs14.at[d], dev(zd, xl, c, y, xh)).start()
    for i in range(3):
        landed(zin.at[i], rs11.at[i])
    for e in range(2):
        for a in range(2):
            t = zsum[3, e, a].astype(F32)
            for i in range(3):
                t = t + zin[i, e, a].astype(F32)
            part[e, a] = t.astype(BF16)
    for n, xld, xhd in x_mates:
        remote(part.at[xhd, xld], pin.at[n], ss10.at[n], rs10.at[n], dev(z, xld, c, y, xhd)).start()
    finish_q(2)

    upper, lower = part[xh, xl].astype(F32), hsum[z].astype(F32)
    for n in (1, 2, 3):
        landed(hin.at[n], rs14.at[n])
        lower = lower + hin[n].astype(F32)
    for n in (1, 2, 3):
        landed(pin.at[n], rs10.at[n])
        upper = upper + pin[n].astype(F32)
    redb[:48, :] = upper.astype(BF16)
    redb[48:, :] = lower.astype(BF16)

    def gw_cols(zs, e):
        return gw_out.at[:, pl.ds(m128((zs * 2 + e) * GW), GW)]

    own = z * 2 + xh
    for n in range(8):
        d, e = n // 2, n % 2
        yd, xd = (y + d) % 4, (xh + e) % 2

        def to_owner():
            remote(redb, gw_cols(z, xh), ss6.at[n], rs6.at[own], dev(y, xl, c, yd, xd)).start()

        if n == 0:
            pl.when(z != y)(to_owner)

            @pl.when(z == y)
            def _():
                local_copy(redb, gw_cols(z, xh), rs6.at[own]).start()
        else:
            to_owner()

    landed(q_cols(y), ls7.at[0])
    for d in (1, 2, 3):
        landed(q_cols((y + 4 - d) % 4), rs7.at[d - 1])

    def collect(hh, carry):
        for t in range(2):
            i = hh * 2 + t
            out = (gk_out, gv_out)[t]
            for d in (1, 2, 3):
                landed(back_slot(out, hh, (y + 4 - d) % 4), rs9.at[i * 3 + d - 1])
            landed(back_slot(out, hh, y), ls9.at[i])
        return carry

    lax.fori_loop(0, 3, collect, 0)
    for n in range(8):
        landed(gw_cols(n // 2, n % 2), rs6.at[n])

    @pl.when(z == y)
    def _():
        for n in range(3):
            landed(w_hbm, ssw1.at[n])

    for n in range(3):
        landed(w_own, ssw2.at[n])

    def left_head(hh, carry):
        for t in range(3):
            for d in (1, 2, 3):
                landed(slot(t, hh, y), ss1.at[(hh * 3 + t) * 3 + d - 1])
        landed(q_half(hh, xh), ss2.at[hh])
        landed(oxs.at[hh], ss4.at[hh])
        landed(sxs.at[hh], ss4.at[hh + 3])
        for t in range(2):
            for d in (1, 2, 3):
                landed(fin.at[hh, 0:TOK, :], ss9.at[(hh * 2 + t) * 3 + d - 1])
        return carry

    lax.fori_loop(0, 3, left_head, 0)
    for n in range(6):
        landed(go_slot(y, 0), ss3.at[n])
    for n in range(4):
        for hh in range(3):
            landed(gxs.at[n, hh], ss8.at[n * 3 + hh])
            landed(cxs.at[n, hh], ss8.at[n * 3 + hh + 12])
        landed(dqxs.at[n], ss12.at[n])
        landed(cin.at[n], ss5.at[n])
    for n in range(3):
        landed(finq.at[n], ss7.at[n])
        landed(zin.at[n], ss11.at[n])
        landed(pin.at[0], ss10.at[n + 1])
        landed(xin.at[0], ss13.at[n + 1])
        landed(hin.at[0], ss14.at[n + 1])

    @pl.when(z != y)
    def _():
        landed(redb, ss6.at[0])

    for n in range(1, 8):
        landed(redb, ss6.at[n])


def store(gq, gk, gv, gw, gq_out, gk_out, gv_out, gw_out):
    gq_out[...] = gq[...]
    gk_out[...] = gk[...]
    gv_out[...] = gv[...]
    gw_out[...] = gw[...].astype(F32)


def local(query_rows, key_rows, value_rows, grad_out, w_out):
    any_spec = pl.BlockSpec(memory_space=pl.ANY)
    dma = pltpu.SemaphoreType.DMA
    vm = pltpu.VMEM
    rows = jax.ShapeDtypeStruct((1, TOK, HW), BF16)
    gq, gk, gv, gw = pl.pallas_call(
        kernel,
        out_shape=(rows, rows, rows, jax.ShapeDtypeStruct((96, D), BF16)),
        in_specs=[any_spec] * 5,
        out_specs=(any_spec,) * 4,
        scratch_shapes=[
            vm((3, 2 * HALF, HD), BF16),
            vm((3, HALF, HD), BF16),
            vm((3, HALF, HD), BF16),
            vm((3, HD, HALF), BF16),
            vm((3, HD, HALF), BF16),
            vm((HALF, D), BF16),
            vm((GW, D), BF16),
            vm((HALF, TOK), F32),
            vm((24, HALF, TOK), BF16),
            vm((GW, HALF), BF16),
            vm((3, 4, HD, TOK), F32),
            vm((3, 4, 8, TOK), F32),
            vm((3, 4, 8, TOK), F32),
            vm((3, 4, HD, TOK), BF16),
            vm((3, 4, HD, TOK), BF16),
            vm((3, 4, 8, TOK), F32),
            vm((3, 4, 8, TOK), F32),
            vm((4, 3, HD, TOK), BF16),
            vm((4, 3, 8, TOK), F32),
            vm((4, 3, HD, TOK), BF16),
            vm((4, 3, HD, TOK), BF16),
            vm((4, 3, 8, TOK), F32),
            vm((4, 3, 8, TOK), F32),
            vm((4, TOK, GW), F32),
            vm((4, TOK, GW), BF16),
            vm((4, TOK, GW), BF16),
            vm((4, TOK, GW), BF16),
            vm((3, HALF, HD), F32),
            vm((3, HALF, HD), F32),
            vm((6, HALF, HD), BF16),
            vm((4, 2, 2, 2, 96, GW), BF16),
            vm((4, 2, 2, 96, GW), BF16),
            vm((4, 2, 2, 48, GW), BF16),
            vm((3, 2, 2, 48, GW), BF16),
            vm((2, 2, 4, 48, GW), BF16),
            vm((4, 4, 48, GW), BF16),
            vm((4, 48, GW), BF16),
            vm((4, 48, GW), BF16),
            vm((2, 2, 48, GW), BF16),
            vm((4, 48, GW), BF16),
            vm((96, GW), BF16),
            vm((8, GW, GW), F32),
            dma((27,)), dma((27,)), dma((9,)),
            dma((3,)), dma((3,)),
            dma((6,)), dma((6,)), dma((1,)),
            dma((3,)), dma((1,)), dma((3,)), dma((3,)),
            dma((6,)), dma((6,)),
            dma((4,)), dma((4,)),
            dma((8,)), dma((8,)),
            dma((3,)), dma((3,)), dma((1,)),
            dma((24,)), dma((24,)),
            dma((18,)), dma((18,)), dma((6,)),
            dma((4,)), dma((4,)),
            dma((3,)), dma((3,)),
            dma((4,)), dma((4,)),
            dma((4,)), dma((4,)), dma((4,)), dma((4,)),
        ],
        compiler_params=pltpu.CompilerParams(
            has_side_effects=True, collective_id=0, vmem_limit_bytes=60 * 1024 * 1024
        ),
    )(query_rows, key_rows, value_rows, grad_out, w_out)
    half = pl.BlockSpec((1, TOK // 2, HW), lambda i: (0, i, 0))
    part = pl.BlockSpec((48, D), lambda i: (i, 0))
    return pl.pallas_call(
        store,
        out_shape=(rows, rows, rows, jax.ShapeDtypeStruct((96, D), F32)),
        grid=(2,),
        in_specs=[half] * 3 + [part],
        out_specs=[half] * 3 + [part],
    )(gq, gk, gv, gw)


def solution(mesh):
    in_specs = (
        P("fsdp", "rows", None),
        P("fsdp", "rows", None),
        P("fsdp", "rows", None),
        P("fsdp", "rows", None),
        P("fsdp", None),
    )
    out_specs = (
        P("fsdp", "rows", None),
        P("fsdp", "rows", None),
        P("fsdp", "rows", None),
        P("fsdp", None),
    )
    return jax.shard_map(local, mesh=mesh, in_specs=in_specs, out_specs=out_specs, check_vma=False)
```

```python
import math

import jax
import jax.numpy as jnp
from jax import lax
from jax.experimental import pallas as pl
from jax.experimental.pallas import tpu as pltpu
from jax.sharding import PartitionSpec as P

F32 = jnp.float32
BF16 = jnp.bfloat16
MESH = pl.DeviceIdType.MESH
D = 3072
HW = 1536
HD = 128
TOK = 256
GW = 384
HALF = 1024
KC = 256
NK = HALF // KC
SCALE = 1.0 / math.sqrt(HD)
CST = SCALE * math.log2(math.e)


def m128(x):
    return pl.multiple_of(x, 128)


def m256(x):
    return pl.multiple_of(x, 256)


def local_copy(src, dst, sem):
    return pltpu.make_async_copy(src, dst, sem)


def remote(src, dst, send_sem, recv_sem, dev):
    return pltpu.make_async_remote_copy(
        src_ref=src, dst_ref=dst, send_sem=send_sem, recv_sem=recv_sem,
        device_id=dev, device_id_type=MESH,
    )


def landed(ref, sem):
    pltpu.make_async_copy(ref, ref, sem).wait()


def dot(a, b):
    return jnp.dot(a, b, preferred_element_type=F32)


def kernel(
    q_hbm, k_hbm, v_hbm, go_hbm, w_hbm,
    gq_out, gk_out, gv_out, gw_out,
    qbuf, kbuf, vbuf, ktb, vtb, go, wbuf, sbuf, pbuf, att, obuf, stat, rbuf,
    oxs, oxr, sxs, sxr, g1, c1, gxs, gxr, cxs, cxr, dqk, dqxs, dqxr, finq,
    dkacc, dvacc, fin, termb, cin, zsum, zin, part, pin, redb, tacc,
    ss1, rs1, ls1, ss2, rs2, ss3, rs3, lsg, ssw1, rsw1, ssw2, rsw2,
    ss4, rs4, ss5, rs5, ss6, rs6, ss7, rs7, ls7, ss8, rs8, ss9, rs9, ls9,
    ss10, rs10, ss11, rs11, ss12, rs12,
):
    f = lax.axis_index("fsdp")
    r = lax.axis_index("rows")
    z, xl, c = f // 4, (f // 2) % 2, f % 2
    y, xh = r // 2, r % 2
    j = f % 4

    def dev(z_, xl_, c_, y_, xh_):
        return (z_ * 4 + xl_ * 2 + c_, y_ * 2 + xh_)

    def ydev(y_):
        return dev(z, xl, c, y_, xh)

    partner = dev(z, xl, c, y, 1 - xh)
    coremate = dev(z, xl, 1 - c, y, xh)
    ins = (k_hbm, v_hbm, q_hbm)

    def slot(t, hh, ys):
        if t == 2:
            return qbuf.at[hh, pl.ds(m256((xh * 4 + ys) * TOK), TOK), :]
        return (kbuf, vbuf)[t].at[hh, pl.ds(m256(ys * TOK), TOK), :]

    def cols(t, hh, yd):
        return ins[t].at[0, :, pl.ds(m128(yd * GW + hh * HD), HD)]

    def w_rows(n):
        return wbuf.at[pl.ds(pl.multiple_of(n * 96, 32), 96), :]

    w_own = w_rows(j)

    barrier = pltpu.get_barrier_semaphore()

    def hello(d):
        pl.semaphore_signal(barrier, inc=1, device_id=d, device_id_type=MESH)

    for d in (1, 2, 3):
        hello(ydev((y + d) % 4))
        hello(dev(z, xl, c, (y + d) % 4, 1 - xh))
        hello(dev((z + d) % 4, xl, c, y, xh))
        hello(dev(z, (xl + d // 2) % 2, c, y, (xh + d % 2) % 2))
    hello(coremate)
    pl.semaphore_wait(barrier, 13)

    @pl.when(z == y)
    def _():
        local_copy(w_hbm, w_own, rsw1.at[0]).start()
        for dz in (1, 2, 3):
            remote(w_hbm, w_own, ssw1.at[dz - 1], rsw1.at[0], dev((z + dz) % 4, xl, c, y, xh)).start()

    def send_head(hh, carry):
        for t in (2, 0, 1):
            for d in (1, 3, 2):
                yd = (y + d) % 4
                i = (hh * 3 + t) * 3 + d - 1
                remote(cols(t, hh, yd), slot(t, hh, y), ss1.at[i], rs1.at[i], ydev(yd)).start()
            local_copy(cols(t, hh, y), slot(t, hh, y), ls1.at[hh * 3 + t]).start()
        return carry

    lax.fori_loop(0, 3, send_head, 0)

    def go_slot(ys, h, n=1):
        return go.at[pl.ds(pl.multiple_of(ys * TOK + h * 128, 128), 128 * n), :]

    def go_src(h):
        return go_hbm.at[0, pl.ds(h * 128, 128), :]

    yr, yl = (y + 1) % 4, (y + 3) % 4
    yo = (y + 2) % 4
    remote(go_src(0), go_slot(y, 0), ss3.at[0], rs3.at[0], ydev(yr)).start()
    remote(go_src(1), go_slot(y, 1), ss3.at[2], rs3.at[2], ydev(yl)).start()
    remote(go_src(1), go_slot(y, 1), ss3.at[1], rs3.at[1], ydev(yr)).start()
    remote(go_src(0), go_slot(y, 0), ss3.at[3], rs3.at[3], ydev(yl)).start()
    local_copy(go_hbm.at[0], go_slot(y, 0, 2), lsg.at[0]).start()

    def arrived(t, hh):
        local_copy(cols(t, hh, y), slot(t, hh, y), ls1.at[hh * 3 + t]).wait()
        for d in (1, 3, 2):
            landed(slot(t, hh, (y + 4 - d) % 4), rs1.at[(hh * 3 + t) * 3 + d - 1])

    def q_half(hh, h):
        return qbuf.at[hh, pl.ds(pl.multiple_of(h * HALF, HALF), HALF), :]

    def relay(hh, carry):
        arrived(2, hh)
        remote(q_half(hh, xh), q_half(hh, xh), ss2.at[hh], rs2.at[hh], partner).start()
        return carry

    lax.fori_loop(0, 3, relay, 0)

    landed(w_own, rsw1.at[0])
    remote(w_own, w_own, ssw2.at[0], rsw2.at[0], coremate).start()
    remote(w_own, w_own, ssw2.at[1], rsw2.at[1], dev(z, 1 - xl, c, y, xh)).start()

    def scores_block(hh, s):
        i = hh * 8 + s
        qt = qbuf[hh, pl.ds(m256(s * TOK), TOK), :].T
        m = jnp.full((1, TOK), -jnp.inf, F32)
        for kc in range(NK):
            ks = slice(kc * KC, (kc + 1) * KC)
            sc = dot(kbuf[hh, ks, :], qt)
            sbuf[ks, :] = sc
            m = jnp.maximum(m, jnp.max(sc, axis=0, keepdims=True))
        mc = m * CST
        l = jnp.zeros((1, TOK), F32)
        o = jnp.zeros((HD, TOK), F32)
        for kc in range(NK):
            ks = slice(kc * KC, (kc + 1) * KC)
            p = jnp.exp2(sbuf[ks, :] * CST - mc)
            l = l + jnp.sum(p, axis=0, keepdims=True)
            pb = p.astype(BF16)
            pbuf[i, ks, :] = pb
            o = o + dot(vtb[hh, :, ks], pb)
        return m, l, o

    def forward(hh, carry):
        arrived(0, hh)
        arrived(1, hh)
        for kc in range(NK):
            ks = slice(kc * KC, (kc + 1) * KC)
            ktb[hh, :, ks] = kbuf[hh, ks, :].T
            vtb[hh, :, ks] = vbuf[hh, ks, :].T
        landed(q_half(hh, 1 - xh), rs2.at[hh])

        def theirs(ys, carry):
            m, l, o = scores_block(hh, (1 - xh) * 4 + ys)
            oxs[hh, ys] = o.astype(BF16)
            sxs[hh, ys, 0:1, :] = m
            sxs[hh, ys, 1:2, :] = l
            return carry

        lax.fori_loop(0, 4, theirs, 0)
        remote(oxs.at[hh], oxr.at[hh], ss4.at[hh], rs4.at[hh], partner).start()
        remote(sxs.at[hh], sxr.at[hh], ss4.at[hh + 3], rs4.at[hh + 3], partner).start()

        def mine(ys, carry):
            m, l, o = scores_block(hh, xh * 4 + ys)
            obuf[hh, ys] = o
            stat[hh, ys, 0:1, :] = m
            stat[hh, ys, 1:2, :] = l
            return carry

        return lax.fori_loop(0, 4, mine, carry)

    lax.fori_loop(0, 3, forward, 0)

    w_across = w_rows((1 - xl) * 2 + c)
    landed(w_across, rsw2.at[1])
    remote(w_across, w_across, ssw2.at[2], rsw2.at[2], coremate).start()

    def merge(hh, carry):
        landed(oxr.at[hh], rs4.at[hh])
        landed(sxr.at[hh], rs4.at[hh + 3])

        def block(ys, carry):
            ma, la = stat[hh, ys, 0:1, :], stat[hh, ys, 1:2, :]
            mb, lb = sxr[hh, ys, 0:1, :], sxr[hh, ys, 1:2, :]
            m = jnp.maximum(ma, mb)
            ea, eb = jnp.exp2((ma - m) * CST), jnp.exp2((mb - m) * CST)
            inv = 1.0 / (la * ea + lb * eb)
            ra, rb = ea * inv, eb * inv
            o = obuf[hh, ys] * ra + oxr[hh, ys].astype(F32) * rb
            obuf[hh, ys] = o
            att[pl.ds(m128(hh * HD), HD), pl.ds(m256(ys * TOK), TOK)] = o.astype(BF16)
            rbuf[hh, ys, 0:1, :] = ra
            rbuf[hh, ys, 1:2, :] = rb
            return carry

        return lax.fori_loop(0, 4, block, carry)

    lax.fori_loop(0, 3, merge, 0)
    landed(w_rows(xl * 2 + 1 - c), rsw2.at[0])
    landed(w_rows((1 - xl) * 2 + 1 - c), rsw2.at[2])

    def project(ys):
        g = lax.dot_general(
            wbuf[...], go[pl.ds(m256(ys * TOK), TOK), :], (((1,), (1,)), ((), ())), preferred_element_type=F32
        )
        for hh in range(3):
            gh = g[hh * HD : (hh + 1) * HD, :]
            cen = jnp.sum(gh * obuf[hh, ys], axis=0, keepdims=True)
            ra, rb = rbuf[hh, ys, 0:1, :], rbuf[hh, ys, 1:2, :]
            g1[ys, hh] = (gh * ra).astype(BF16)
            gxs[ys, hh] = (gh * rb).astype(BF16)
            c1[ys, hh, 0:1, :] = cen * ra
            cxs[ys, hh, 0:1, :] = cen * rb
            i = ys * 3 + hh
            remote(gxs.at[ys, hh], gxr.at[ys, hh], ss8.at[i], rs8.at[i], partner).start()
            remote(cxs.at[ys, hh], cxr.at[ys, hh], ss8.at[i + 12], rs8.at[i + 12], partner).start()

    dkacc[...] = jnp.zeros_like(dkacc)
    dvacc[...] = jnp.zeros_like(dvacc)

    def one_head(own, ys, hh):
        s = (xh if own else 1 - xh) * 4 + ys
        i = hh * 8 + s
        qn = qbuf[hh, pl.ds(m256(s * TOK), TOK), :]
        gt = (g1 if own else gxr)[ys, hh]
        cen = (c1 if own else cxr)[ys, hh, 0:1, :]
        gn = gt.T
        dq = jnp.zeros((HD, TOK), F32)
        for kc in range(NK):
            ks = slice(kc * KC, (kc + 1) * KC)
            dp = dot(vbuf[hh, ks, :], gt)
            pb = pbuf[i, ks, :]
            ds = (pb.astype(F32) * (dp - cen)).astype(BF16)
            dq = dq + dot(ktb[hh, :, ks], ds)
            dkacc[hh, ks, :] += dot(ds, qn)
            dvacc[hh, ks, :] += dot(pb, gn)
        dqn = (dq * SCALE).T
        hs = pl.ds(m128(hh * HD), HD)
        if own:
            dqk[ys, :, hs] = dqn
        else:
            dqxs[ys, :, hs] = dqn.astype(BF16)

    def head_in(ys, hh):
        i = ys * 3 + hh
        landed(gxr.at[ys, hh], rs8.at[i])
        landed(cxr.at[ys, hh], rs8.at[i + 12])

    def backward(own, ys):
        def head(hh, carry):
            one_head(own, ys, hh)
            return carry

        lax.fori_loop(0, 3, head, 0)

    def theirs_in(ys):
        for hh in range(3):
            head_in(ys, hh)

    def send_dq(ys):
        remote(dqxs.at[ys], dqxr.at[ys], ss12.at[ys], rs12.at[ys], partner).start()

    def q_cols(ysrc):
        return gq_out.at[0, :, pl.ds(m128(ysrc * GW), GW)]

    def finish_q(d):
        ys = (y + d) % 4
        landed(dqxr.at[ys], rs12.at[ys])
        finq[ys] = (dqk[ys] + dqxr[ys].astype(F32)).astype(BF16)
        if d == 0:
            local_copy(finq.at[ys], q_cols(y), ls7.at[0]).start()
        else:
            remote(finq.at[ys], q_cols(y), ss7.at[d - 1], rs7.at[d - 1], ydev(ys)).start()

    local_copy(go_hbm.at[0], go_slot(y, 0, 2), lsg.at[0]).wait()
    project(y)
    backward(True, y)

    landed(go_slot(yl, 0), rs3.at[0])
    remote(go_slot(yl, 0), go_slot(yl, 0), ss3.at[4], rs3.at[4], ydev(yr)).start()
    landed(go_slot(yr, 1), rs3.at[2])
    remote(go_slot(yr, 1), go_slot(yr, 1), ss3.at[5], rs3.at[5], ydev(yl)).start()

    theirs_in(y)
    backward(False, y)
    send_dq(y)

    def term_cols(zd, xd):
        return pl.ds(m128((zd * 2 + xd) * GW), GW)

    def term_dot(ys, zd, xd):
        at = pl.ds(m256(ys * TOK), TOK)
        return dot(att[:, at], go[at, term_cols(zd, xd)])

    def term_part(ys, first=False):
        def add(n, carry):
            t = term_dot(ys, n // 2, n % 2)
            tacc[n] = t if first else tacc[n] + t
            return carry

        lax.fori_loop(0, 8, add, 0)

    term_part(y, True)
    landed(go_slot(yl, 1), rs3.at[1])
    project(yl)
    backward(True, yl)
    landed(go_slot(yr, 0), rs3.at[3])
    project(yr)
    theirs_in(yl)
    backward(False, yl)
    send_dq(yl)
    backward(True, yr)
    theirs_in(yr)
    backward(False, yr)
    send_dq(yr)
    term_part(yl)
    term_part(yr)
    finish_q(0)
    finish_q(3)
    finish_q(1)

    landed(go_slot(yo, 0), rs3.at[4])
    landed(go_slot(yo, 1), rs3.at[5])
    project(yo)

    def term(o, carry):
        zd = (z + 1 + o) % 4
        for xd in range(2):
            t = (tacc[zd * 2 + xd] + term_dot(yo, zd, xd)).astype(BF16)
            for n in range(4):
                termb[zd, n % 2, xd, n // 2] = t[n * 96 : (n + 1) * 96, :]
        remote(termb.at[zd, 1 - c], cin.at[zd], ss5.at[zd], rs5.at[zd], coremate).start()
        return carry

    lax.fori_loop(0, 4, term, 0)

    def back_slot(out, hh, ysrc):
        return out.at[0, :, pl.ds(m128(ysrc * GW + hh * HD), HD)]

    def hand_out(hh):
        for t in range(2):
            i = hh * 2 + t
            fin[i] = ((dkacc, dvacc)[t][hh] * (SCALE, 1.0)[t]).astype(BF16)
            out = (gk_out, gv_out)[t]
            for d in (1, 3, 2):
                yd = (y + d) % 4
                n = i * 3 + d - 1
                remote(fin.at[i, pl.ds(m256(yd * TOK), TOK), :], back_slot(out, hh, y), ss9.at[n], rs9.at[n],
                       ydev(yd)).start()
            local_copy(fin.at[i, pl.ds(m256(y * TOK), TOK), :], back_slot(out, hh, y), ls9.at[i]).start()

    backward(True, yo)

    def to_z(o, carry):
        zd = (z + 1 + o) % 4
        landed(cin.at[zd], rs5.at[zd])
        for e in range(2):
            for a in range(2):
                t = termb[zd, c, e, a].astype(F32) + cin[zd, e, a].astype(F32)
                zsum[o, e, a] = t.astype(BF16)

        @pl.when(o < 3)
        def _():
            remote(zsum.at[o], zin.at[o], ss11.at[o], rs11.at[o], dev(zd, xl, c, y, xh)).start()

        return carry

    lax.fori_loop(0, 4, to_z, 0)


    def last_head(hh, carry):
        head_in(yo, hh)
        one_head(False, yo, hh)
        hand_out(hh)
        return carry

    lax.fori_loop(0, 3, last_head, 0)
    send_dq(yo)

    for i in range(3):
        landed(zin.at[i], rs11.at[i])
    for e in range(2):
        for a in range(2):
            t = zsum[3, e, a].astype(F32)
            for i in range(3):
                t = t + zin[i, e, a].astype(F32)
            part[e, a] = t.astype(BF16)
    for n in (1, 2, 3):
        a, e = n // 2, n % 2
        xld, xhd = (xl + a) % 2, (xh + e) % 2
        remote(part.at[xhd, xld], pin.at[n], ss10.at[n], rs10.at[n], dev(z, xld, c, y, xhd)).start()
    finish_q(2)

    acc = part[xh, xl].astype(F32)
    for n in (1, 2, 3):
        landed(pin.at[n], rs10.at[n])
        acc = acc + pin[n].astype(F32)
    redb[...] = acc.astype(BF16)

    def gw_cols(zs, e):
        return gw_out.at[:, pl.ds(m128((zs * 2 + e) * GW), GW)]

    own = z * 2 + xh
    for n in range(8):
        d, e = n // 2, n % 2
        yd, xd = (y + d) % 4, (xh + e) % 2

        def to_owner():
            remote(redb, gw_cols(z, xh), ss6.at[n], rs6.at[own], dev(y, xl, c, yd, xd)).start()

        if n == 0:
            pl.when(z != y)(to_owner)

            @pl.when(z == y)
            def _():
                local_copy(redb, gw_cols(z, xh), rs6.at[own]).start()
        else:
            to_owner()

    landed(q_cols(y), ls7.at[0])
    for d in (1, 2, 3):
        landed(q_cols((y + 4 - d) % 4), rs7.at[d - 1])

    def collect(hh, carry):
        for t in range(2):
            i = hh * 2 + t
            out = (gk_out, gv_out)[t]
            for d in (1, 2, 3):
                landed(back_slot(out, hh, (y + 4 - d) % 4), rs9.at[i * 3 + d - 1])
            landed(back_slot(out, hh, y), ls9.at[i])
        return carry

    lax.fori_loop(0, 3, collect, 0)
    for n in range(8):
        landed(gw_cols(n // 2, n % 2), rs6.at[n])

    @pl.when(z == y)
    def _():
        for n in range(3):
            landed(w_hbm, ssw1.at[n])

    for n in range(3):
        landed(w_own, ssw2.at[n])

    def left_head(hh, carry):
        for t in range(3):
            for d in (1, 2, 3):
                landed(slot(t, hh, y), ss1.at[(hh * 3 + t) * 3 + d - 1])
        landed(q_half(hh, xh), ss2.at[hh])
        landed(oxs.at[hh], ss4.at[hh])
        landed(sxs.at[hh], ss4.at[hh + 3])
        for t in range(2):
            for d in (1, 2, 3):
                landed(fin.at[hh, 0:TOK, :], ss9.at[(hh * 2 + t) * 3 + d - 1])
        return carry

    lax.fori_loop(0, 3, left_head, 0)
    for n in range(6):
        landed(go_slot(y, 0), ss3.at[n])
    for n in range(4):
        for hh in range(3):
            landed(gxs.at[n, hh], ss8.at[n * 3 + hh])
            landed(cxs.at[n, hh], ss8.at[n * 3 + hh + 12])
        landed(dqxs.at[n], ss12.at[n])
        landed(cin.at[n], ss5.at[n])
    for n in range(3):
        landed(finq.at[n], ss7.at[n])
        landed(zin.at[n], ss11.at[n])
        landed(pin.at[0], ss10.at[n + 1])

    @pl.when(z != y)
    def _():
        landed(redb, ss6.at[0])

    for n in range(1, 8):
        landed(redb, ss6.at[n])


def store(gq, gk, gv, gw, gq_out, gk_out, gv_out, gw_out):
    gq_out[...] = gq[...]
    gk_out[...] = gk[...]
    gv_out[...] = gv[...]
    gw_out[...] = gw[...].astype(F32)


def local(query_rows, key_rows, value_rows, grad_out, w_out):
    any_spec = pl.BlockSpec(memory_space=pl.ANY)
    dma = pltpu.SemaphoreType.DMA
    vm = pltpu.VMEM
    rows = jax.ShapeDtypeStruct((1, TOK, HW), BF16)
    gq, gk, gv, gw = pl.pallas_call(
        kernel,
        out_shape=(rows, rows, rows, jax.ShapeDtypeStruct((96, D), BF16)),
        in_specs=[any_spec] * 5,
        out_specs=(any_spec,) * 4,
        scratch_shapes=[
            vm((3, 2 * HALF, HD), BF16),
            vm((3, HALF, HD), BF16),
            vm((3, HALF, HD), BF16),
            vm((3, HD, HALF), BF16),
            vm((3, HD, HALF), BF16),
            vm((HALF, D), BF16),
            vm((GW, D), BF16),
            vm((HALF, TOK), F32),
            vm((24, HALF, TOK), BF16),
            vm((GW, HALF), BF16),
            vm((3, 4, HD, TOK), F32),
            vm((3, 4, 8, TOK), F32),
            vm((3, 4, 8, TOK), F32),
            vm((3, 4, HD, TOK), BF16),
            vm((3, 4, HD, TOK), BF16),
            vm((3, 4, 8, TOK), F32),
            vm((3, 4, 8, TOK), F32),
            vm((4, 3, HD, TOK), BF16),
            vm((4, 3, 8, TOK), F32),
            vm((4, 3, HD, TOK), BF16),
            vm((4, 3, HD, TOK), BF16),
            vm((4, 3, 8, TOK), F32),
            vm((4, 3, 8, TOK), F32),
            vm((4, TOK, GW), F32),
            vm((4, TOK, GW), BF16),
            vm((4, TOK, GW), BF16),
            vm((4, TOK, GW), BF16),
            vm((3, HALF, HD), F32),
            vm((3, HALF, HD), F32),
            vm((6, HALF, HD), BF16),
            vm((4, 2, 2, 2, 96, GW), BF16),
            vm((4, 2, 2, 96, GW), BF16),
            vm((4, 2, 2, 96, GW), BF16),
            vm((3, 2, 2, 96, GW), BF16),
            vm((2, 2, 96, GW), BF16),
            vm((4, 96, GW), BF16),
            vm((96, GW), BF16),
            vm((8, GW, GW), F32),
            dma((27,)), dma((27,)), dma((9,)),
            dma((3,)), dma((3,)),
            dma((6,)), dma((6,)), dma((1,)),
            dma((3,)), dma((1,)), dma((3,)), dma((3,)),
            dma((6,)), dma((6,)),
            dma((4,)), dma((4,)),
            dma((8,)), dma((8,)),
            dma((3,)), dma((3,)), dma((1,)),
            dma((24,)), dma((24,)),
            dma((18,)), dma((18,)), dma((6,)),
            dma((4,)), dma((4,)),
            dma((3,)), dma((3,)),
            dma((4,)), dma((4,)),
        ],
        compiler_params=pltpu.CompilerParams(
            has_side_effects=True, collective_id=0, vmem_limit_bytes=60 * 1024 * 1024
        ),
    )(query_rows, key_rows, value_rows, grad_out, w_out)
    half = pl.BlockSpec((1, TOK // 2, HW), lambda i: (0, i, 0))
    part = pl.BlockSpec((48, D), lambda i: (i, 0))
    return pl.pallas_call(
        store,
        out_shape=(rows, rows, rows, jax.ShapeDtypeStruct((96, D), F32)),
        grid=(2,),
        in_specs=[half] * 3 + [part],
        out_specs=[half] * 3 + [part],
    )(gq, gk, gv, gw)


def solution(mesh):
    in_specs = (
        P("fsdp", "rows", None),
        P("fsdp", "rows", None),
        P("fsdp", "rows", None),
        P("fsdp", "rows", None),
        P("fsdp", None),
    )
    out_specs = (
        P("fsdp", "rows", None),
        P("fsdp", "rows", None),
        P("fsdp", "rows", None),
        P("fsdp", None),
    )
    return jax.shard_map(local, mesh=mesh, in_specs=in_specs, out_specs=out_specs, check_vma=False)
```
